512 devices in a mesh: row: 16 (over z, y_lo), col: 4 (over x), seq: 8 (over y_hi, core).
Axes of the slice: x: 4, y: 8 (y_hi: 4, y_lo: 2; y = y_hi * 2 + y_lo), z: 8, core: 2. Of those that a mesh axis runs over, the one named last changes fastest.
Arguments:
- pair: bfloat16 [1024, 1024, 128], P(('row', 'seq'), 'col'), may hold values from -6 to 6
- alignment: bfloat16 [128, 1024, 256], P(('row', 'seq'), 'col'), may hold values from -6 to 6
- opm_left: bfloat16 [256, 32], replicated, may hold values from -0.375 to 0.375
- opm_right: bfloat16 [256, 32], replicated, may hold values from -0.375 to 0.375
- opm_out: bfloat16 [1024, 128], replicated, may hold values from -2 to 2
- tri_left: bfloat16 [128, 128], replicated, may hold values from -0.5 to 0.5
- tri_left_gate: bfloat16 [128, 128], replicated, may hold values from -0.5 to 0.5
- tri_right: bfloat16 [128, 128], replicated, may hold values from -0.5 to 0.5
- tri_right_gate: bfloat16 [128, 128], replicated, may hold values from -0.5 to 0.5
- tri_gate: bfloat16 [128, 128], replicated, may hold values from -0.5 to 0.5
- tri_out: bfloat16 [128, 128], replicated, may hold values from -0.5 to 0.5
Outputs:
- pair_out: bfloat16 [1024, 1024, 128], P(('row', 'seq'), 'col')
The draws below stay inside these ranges and needn't reach their ends.
All inputs are finite; a program needn't handle non-finite values.
Results may differ from the reference program's by a relative error of at most 0.0075.
Values may be sent and summed in bfloat16 or wider, within the bound.
A program may use at most 64 MiB of HBM per device.

```python
import jax
import jax.numpy as jnp
from jax import lax

CZ = 128
CM = 256
CO = 32
CH = 128
SEQS = 128
NRES = 1024


def level_of(stream_key, dims, split, least, high):
    factor_of = 1.0
    for dim, blocks in split:
        steps = jax.random.uniform(jax.random.fold_in(jax.random.fold_in(stream_key, 6), dim), (blocks,), jnp.float32, least / len(split), high / len(split))
        factor_of = factor_of * jnp.repeat(jnp.exp(steps), dims[dim] // blocks).reshape((-1,) + (1,) * (len(dims) - 1 - dim))
    return factor_of


def bell_draw(rng, dims, width, limit, shards=(), held_as=jnp.bfloat16):
    loudness = level_of(rng, dims, shards, -0.22, 0.18) if shards else 1.0
    drawn = jax.random.normal(rng, dims, jnp.float32) * width * loudness
    return jnp.minimum(jnp.maximum(drawn, -limit), limit).astype(held_as)


def setup_inputs(seed: int = 0) -> dict:
    key_list = jax.random.split(jax.random.key(seed), 12)
    pair = bell_draw(key_list[0], (NRES, NRES, CZ), 1.0, 6.0, ((0, 128), (1, 4)))
    alignment = bell_draw(key_list[1], (SEQS, NRES, CM), 1.0, 6.0, ((0, 128), (1, 4)))
    opm_left = bell_draw(key_list[2], (CM, CO), CM ** -0.5, 0.375)
    opm_right = bell_draw(key_list[3], (CM, CO), CM ** -0.5, 0.375)
    opm_out = bell_draw(key_list[4], (CO * CO, CZ), 0.35, 2.0)
    tri_left = bell_draw(key_list[5], (CZ, CH), CZ ** -0.5, 0.5)
    tri_left_gate = bell_draw(key_list[6], (CZ, CH), CZ ** -0.5, 0.5)
    tri_right = bell_draw(key_list[7], (CZ, CH), CZ ** -0.5, 0.5)
    tri_right_gate = bell_draw(key_list[8], (CZ, CH), CZ ** -0.5, 0.5)
    tri_gate = bell_draw(key_list[9], (CZ, CZ), CZ ** -0.5, 0.5)
    tri_out = bell_draw(key_list[10], (CH, CZ), CH ** -0.5, 0.5)
    return dict(pair=pair, alignment=alignment, opm_left=opm_left, opm_right=opm_right, opm_out=opm_out, tri_left=tri_left, tri_left_gate=tri_left_gate, tri_right=tri_right, tri_right_gate=tri_right_gate, tri_gate=tri_gate, tri_out=tri_out)


EPS = 1e-05

def layer_norm(values, axis):
    values = values.astype(jnp.float32)
    center = values - lax.optimization_barrier(jnp.mean(values, axis=axis, keepdims=True))
    spread = lax.optimization_barrier(jnp.mean(center * center, axis=axis, keepdims=True))
    return center * lax.rsqrt(spread + EPS)

def reference(pair, alignment, opm_left, opm_right, opm_out, tri_left, tri_left_gate, tri_right, tri_right_gate, tri_gate, tri_out):
    seq_normed = layer_norm(alignment, 2).astype(jnp.bfloat16).reshape(SEQS * NRES, CM)
    left_factor = jnp.dot(seq_normed, opm_left, preferred_element_type=jnp.float32).astype(jnp.bfloat16).reshape(SEQS, NRES, CO)
    right_factor = jnp.dot(seq_normed, opm_right, preferred_element_type=jnp.float32).astype(jnp.bfloat16).reshape(SEQS, NRES, CO)
    right_wide = right_factor.astype(jnp.float32)

    def outer_row(packed):
        row_vals, pair_row = packed
        outer_sum = jnp.einsum('np,njq->jpq', row_vals.astype(jnp.float32), right_wide)
        mean_outer = (outer_sum * (1.0 / SEQS)).astype(jnp.bfloat16).reshape(NRES, CO * CO)
        return (pair_row.astype(jnp.float32) + jnp.dot(mean_outer, opm_out, preferred_element_type=jnp.float32)).astype(jnp.bfloat16)
    pair_mid = lax.map(outer_row, (jnp.swapaxes(left_factor, 0, 1), pair))
    normed_pair = layer_norm(pair_mid, 2).astype(jnp.bfloat16)
    flat_pair = normed_pair.reshape(NRES * NRES, CZ)

    def gated(weight_gate, weight_value):
        gate_part = jax.nn.sigmoid(jnp.dot(flat_pair, weight_gate, preferred_element_type=jnp.float32))
        value_part = jnp.dot(flat_pair, weight_value, preferred_element_type=jnp.float32)
        return (gate_part * value_part).astype(jnp.bfloat16).reshape(NRES, NRES, CH)
    left_tri = jnp.transpose(gated(tri_left_gate, tri_left), (2, 0, 1))
    right_tri = jnp.transpose(gated(tri_right_gate, tri_right), (2, 0, 1))

    def channel(packed):
        left_chan, right_chan = packed
        return jnp.dot(left_chan, right_chan.T, preferred_element_type=jnp.float32).astype(jnp.bfloat16)
    product = lax.map(channel, (left_tri, right_tri))
    product_last = jnp.transpose(product, (1, 2, 0))

    def finish(packed):
        product_row, normed_row, pair_row = packed
        normed_product = layer_norm(product_row, 1).astype(jnp.bfloat16)
        update = jnp.dot(normed_product, tri_out, preferred_element_type=jnp.float32)
        gate_part = jax.nn.sigmoid(jnp.dot(normed_row, tri_gate, preferred_element_type=jnp.float32))
        return (pair_row.astype(jnp.float32) + gate_part * update).astype(jnp.bfloat16)
    return lax.map(finish, (product_last, normed_pair, pair_mid))
```

```python
import functools

import jax
import jax.numpy as jnp
from jax import lax
from jax.experimental import pallas as pl
from jax.experimental.pallas import tpu as pltpu
from jax.sharding import PartitionSpec as P

EPS = 1e-05
MESH = pl.DeviceIdType.MESH
F32 = jnp.float32
BF16 = jnp.bfloat16
VMEM = pl.BlockSpec(memory_space=pltpu.VMEM)
ANY = pl.BlockSpec(memory_space=pl.ANY)
DMA = pltpu.SemaphoreType.DMA

NX = 4
NZ = 8
NQ = 8
NS = 2 * NQ
NY = NS // 2
HOPS = (1, 7, 2, 6, 3, 5, 4)


class Place:
    def __init__(self):
        row = lax.axis_index("row")
        self.x = lax.axis_index("col")
        seq = lax.axis_index("seq")
        self.z = row // 2
        self.s = (row % 2) * NQ + seq
        self.yy = self.s // 2
        self.core = self.s % 2

    def at(self, z=None, s=None, x=None):
        z = self.z if z is None else z
        s = self.s if s is None else s
        x = self.x if x is None else x
        return (z * 2 + s // NQ, x, s % NQ)


def send(src, dst, send_sem, recv_sem, device):
    pltpu.make_async_remote_copy(
        src_ref=src,
        dst_ref=dst,
        send_sem=send_sem,
        recv_sem=recv_sem,
        device_id=device,
        device_id_type=MESH,
    ).start()


def keep(src, dst, sem):
    pltpu.make_async_copy(src, dst, sem).start()


def await_bytes(ref, sem):
    pltpu.make_async_copy(ref, ref, sem).wait()


def greet(device):
    pl.semaphore_signal(
        pltpu.get_barrier_semaphore(), inc=1, device_id=device, device_id_type=MESH
    )


def greet_plane(me):
    for t in range(1, NS):
        greet(me.at(s=(me.s + t) % NS))
    for t in range(1, NZ):
        greet(me.at(z=(me.z + t) % NZ))
    return NS - 1 + NZ - 1


def layer_norm(values, axis):
    values = values.astype(F32)
    center = values - jnp.mean(values, axis=axis, keepdims=True)
    spread = jnp.mean(center * center, axis=axis, keepdims=True)
    return center * lax.rsqrt(spread + EPS)


def gather_kernel(
    right_ref, left_ref, all_ref, mine_ref, half_ref, send_sem, first_sem, next_sem, twin_sem, left_sem
):
    me = Place()
    z, s, x, yy, core = me.z, me.s, me.x, me.yy, me.core
    owner = z // 2

    count = greet_plane(me)
    for t in range(NZ):

        @pl.when(jnp.logical_not(jnp.logical_and(owner == x, z == t)))
        def _():
            greet(me.at(z=t, x=owner))

    here = jnp.where(owner == x, 1, 0)
    pl.semaphore_wait(pltpu.get_barrier_semaphore(), count + 8 - here)

    for h in range(2):
        for xt in range(NX):
            zt = 2 * x + h
            same = jnp.logical_and(x == xt, z == zt)

            @pl.when(same)
            def _():
                keep(left_ref.at[h], half_ref.at[z], left_sem.at[0])

            @pl.when(jnp.logical_not(same))
            def _():
                send(
                    left_ref.at[h], half_ref.at[z], send_sem.at[0], left_sem.at[0], me.at(z=zt, x=xt)
                )

    own = all_ref.at[z, yy, core]
    keep(right_ref, own, first_sem)

    @pl.when(core == 0)
    def _():
        for t in HOPS:
            send(right_ref, own, send_sem.at[1], first_sem, me.at(z=(z + t) % NZ))

    @pl.when(core == 1)
    def _():
        for t in HOPS:
            send(right_ref, own, send_sem.at[1], first_sem, me.at(s=(s + 2 * t) % NS))

    await_bytes(half_ref, left_sem.at[0])
    keep(half_ref.at[:, s], mine_ref.at[:, s], left_sem.at[1])
    for t in range(1, NS):
        st = (s + t) % NS
        send(half_ref.at[:, st], mine_ref.at[:, s], send_sem.at[2], left_sem.at[1], me.at(s=st))

    await_bytes(all_ref.at[:, 0, 0], first_sem)
    twin = me.at(s=s + 1 - 2 * core)

    @pl.when(core == 0)
    def _():
        line = all_ref.at[:, yy, 0]
        for t in HOPS:
            send(line, line, send_sem.at[3], next_sem.at[yy], me.at(s=(s + 2 * t) % NS))
        send(line, line, send_sem.at[4], twin_sem.at[yy], twin)
        for t in HOPS:
            yt = (yy + t) % NY
            part = all_ref.at[:, yt, 0]
            await_bytes(part, next_sem.at[yt])
            send(part, part, send_sem.at[4], twin_sem.at[yt], twin)

    @pl.when(core == 1)
    def _():
        line = all_ref.at[z, :, 1]
        for t in HOPS:
            send(line, line, send_sem.at[3], next_sem.at[z], me.at(z=(z + t) % NZ))
        send(line, line, send_sem.at[4], twin_sem.at[z], twin)
        for t in HOPS:
            zt = (z + t) % NZ
            part = all_ref.at[zt, :, 1]
            await_bytes(part, next_sem.at[zt])
            send(part, part, send_sem.at[4], twin_sem.at[zt], twin)

    for t in range(8):
        await_bytes(all_ref.at[:, 0, 0], twin_sem.at[t])
    await_bytes(mine_ref, left_sem.at[1])

    @pl.when(here == 1)
    def _():
        await_bytes(half_ref.at[pl.ds(0, 7)], send_sem.at[0])

    @pl.when(here == 0)
    def _():
        await_bytes(half_ref, send_sem.at[0])

    await_bytes(all_ref.at[pl.ds(0, 7), 0, 0], send_sem.at[1])
    await_bytes(mine_ref.at[:, pl.ds(0, NS - 1)], send_sem.at[2])
    await_bytes(all_ref.at[pl.ds(0, 7), :, 0], send_sem.at[3])
    await_bytes(all_ref.at[:, :, 0], send_sem.at[4])


def gather_factors(right, left):
    q, cols = right.shape
    pair = left.shape[2:]
    return pl.pallas_call(
        gather_kernel,
        out_shape=(
            jax.ShapeDtypeStruct((NZ, NY, 2, q, cols), BF16),
            jax.ShapeDtypeStruct((NZ, NS) + pair, BF16),
        ),
        in_specs=[VMEM, VMEM],
        out_specs=(ANY, ANY),
        scratch_shapes=[
            pltpu.VMEM((NZ, NS) + pair, BF16),
            DMA((5,)),
            DMA,
            DMA((8,)),
            DMA((8,)),
            DMA((2,)),
        ],
        compiler_params=pltpu.CompilerParams(collective_id=0, has_side_effects=True),
        name="gather_factors",
    )(right, left)


def first_legs(me, a_in, b_in, a_mid, b_mid, send_sem, a_sem, b_sem):
    z, s = me.z, me.s
    keep(a_in.at[:, s], a_mid.at[s], a_sem)
    keep(b_in.at[z], b_mid.at[z], b_sem)
    for t in range(1, NS):
        st = (s + t) % NS
        send(a_in.at[:, st], a_mid.at[s], send_sem.at[0], a_sem, me.at(s=st))
        if t <= len(HOPS):
            zt = (z + HOPS[t - 1]) % NZ
            send(b_in.at[zt], b_mid.at[z], send_sem.at[1], b_sem, me.at(z=zt))


def sent_legs(a_mid, b_mid, send_sem):
    await_bytes(a_mid.at[pl.ds(0, NS - 1)], send_sem.at[0])
    await_bytes(b_mid.at[pl.ds(0, NZ - 1)], send_sem.at[1])
    await_bytes(a_mid.at[:, pl.ds(0, NZ - 1)], send_sem.at[2])
    await_bytes(b_mid.at[:, pl.ds(0, NS - 1)], send_sem.at[3])


def spread_kernel(
    a_in,
    b_in,
    a_out,
    b_out,
    a_mid,
    b_mid,
    b_all,
    send_sem,
    first_sem,
    a_sem,
    b_sem,
    right_sem,
    left_sem,
    far_sem,
    side_sem,
):
    me = Place()
    z, s, x = me.z, me.s, me.x
    count = greet_plane(me)
    for t in range(1, NX):
        greet(me.at(x=(x + t) % NX))
    pl.semaphore_wait(pltpu.get_barrier_semaphore(), count + NX - 1)

    first_legs(me, a_in, b_in, a_mid, b_mid, send_sem, first_sem.at[0], first_sem.at[1])
    await_bytes(a_mid, first_sem.at[0])
    keep(a_mid.at[:, z], a_out.at[x, z], a_sem.at[z])
    for t in HOPS:
        zt = (z + t) % NZ
        send(a_mid.at[:, zt], a_out.at[x, z], send_sem.at[2], a_sem.at[z], me.at(z=zt))
    await_bytes(b_mid, first_sem.at[1])
    keep(b_mid.at[:, s], b_all.at[:, s], b_sem)
    for t in range(1, NS):
        st = (s + t) % NS
        send(b_mid.at[:, st], b_all.at[:, s], send_sem.at[3], b_sem, me.at(s=st))

    after, before = (x + 1) % NX, (x + 3) % NX

    def pass_on(t):
        zt = (z + t) % NZ
        if t in (0, 5, 6, 7):
            part = a_out.at[before, zt]
            await_bytes(part, left_sem.at[zt])
            send(part, part, send_sem.at[5], far_sem.at[zt], me.at(x=after))
        else:
            part = a_out.at[after, zt]
            await_bytes(part, right_sem.at[zt])
            send(part, part, send_sem.at[5], far_sem.at[zt], me.at(x=before))

    order = (0,) + HOPS
    for k, t in enumerate(order):
        zt = (z + t) % NZ
        part = a_out.at[x, zt]
        await_bytes(part, a_sem.at[zt])
        send(part, part, send_sem.at[4], left_sem.at[zt], me.at(x=after))
        send(part, part, send_sem.at[4], right_sem.at[zt], me.at(x=before))
        if k >= 2:
            pass_on(order[k - 2])
    await_bytes(b_all, b_sem)
    keep(b_all.at[pl.ds(2 * x, 2)], b_out.at[x], side_sem)
    for t in range(1, NX):
        xt = (x + t) % NX
        send(b_all.at[pl.ds(2 * xt, 2)], b_out.at[x], send_sem.at[6], side_sem, me.at(x=xt))
    for t in order[-2:]:
        pass_on(t)
    for t in order:
        zt = (z + t) % NZ
        await_bytes(a_out.at[x, zt], far_sem.at[zt])
        await_bytes(a_out.at[x, zt], (right_sem if t in (0, 5, 6, 7) else left_sem).at[zt])
    await_bytes(b_out, side_sem)

    sent_legs(a_mid, b_mid, send_sem)
    await_bytes(a_out.at[pl.ds(0, 2)], send_sem.at[4])
    await_bytes(a_out.at[0], send_sem.at[5])
    await_bytes(b_out.at[pl.ds(0, NX - 1)], send_sem.at[6])


def spread_triangle(left, right):
    rows, cols = left.shape[2:]
    return pl.pallas_call(
        spread_kernel,
        out_shape=(
            jax.ShapeDtypeStruct((NX, NZ, NS, rows, cols), BF16),
            jax.ShapeDtypeStruct((NX, NZ // NX, NS, rows, cols), BF16),
        ),
        in_specs=[VMEM, VMEM],
        out_specs=(ANY, ANY),
        scratch_shapes=[
            pltpu.VMEM((NS, NZ, rows, cols), BF16),
            pltpu.VMEM((NZ, NS, rows, cols), BF16),
            pltpu.VMEM((NZ, NS, rows, cols), BF16),
            DMA((7,)),
            DMA((2,)),
            DMA((NZ,)),
            DMA,
            DMA((NZ,)),
            DMA((NZ,)),
            DMA((NZ,)),
            DMA,
        ],
        compiler_params=pltpu.CompilerParams(collective_id=1, has_side_effects=True),
        name="spread_triangle",
    )(left, right)


def return_kernel(a_in, b_in, a_out, b_out, a_mid, b_mid, send_sem, first_sem, last_sem):
    me = Place()
    z, s = me.z, me.s
    pl.semaphore_wait(pltpu.get_barrier_semaphore(), greet_plane(me))

    first_legs(me, a_in, b_in, a_mid, b_mid, send_sem, first_sem.at[0], first_sem.at[1])
    await_bytes(a_mid, first_sem.at[0])
    keep(a_mid.at[:, z], a_out.at[z], last_sem.at[0])
    for t in HOPS:
        zt = (z + t) % NZ
        send(a_mid.at[:, zt], a_out.at[z], send_sem.at[2], last_sem.at[0], me.at(z=zt))
    await_bytes(b_mid, first_sem.at[1])
    keep(b_mid.at[:, s], b_out.at[:, s], last_sem.at[1])
    for t in range(1, NS):
        st = (s + t) % NS
        send(b_mid.at[:, st], b_out.at[:, s], send_sem.at[3], last_sem.at[1], me.at(s=st))
    await_bytes(a_out, last_sem.at[0])
    await_bytes(b_out, last_sem.at[1])
    sent_legs(a_mid, b_mid, send_sem)


def return_product(a, b):
    rows, cols = a.shape[2:]
    out = jax.ShapeDtypeStruct((NZ, NS, rows, cols), BF16)
    return pl.pallas_call(
        return_kernel,
        out_shape=(out, out),
        in_specs=[VMEM, VMEM],
        out_specs=(ANY, ANY),
        scratch_shapes=[
            pltpu.VMEM((NS, NZ, rows, cols), BF16),
            pltpu.VMEM((NZ, NS, rows, cols), BF16),
            DMA((4,)),
            DMA((2,)),
            DMA((2,)),
        ],
        compiler_params=pltpu.CompilerParams(collective_id=2, has_side_effects=True),
        name="return_product",
    )(a, b)


def turned(ref):
    return ref[...].astype(F32).T.astype(BF16)


def sigmoid(x):
    return jax.nn.sigmoid(x)


def outer_kernel(
    seqs,
    left_ref,
    right_ref,
    out_ref,
    pair_ref,
    wl_ref,
    wlg_ref,
    wr_ref,
    wrg_ref,
    left_out,
    right_out,
    mid_out,
    normed_out,
    wide,
    stack,
    left_acc,
    right_acc,
):
    rows, cols, width = pair_ref.shape
    factor = left_ref.shape[0] // rows
    halves = cols // 128

    @pl.loop(0, seqs // 8)
    def _(k):
        at = pl.ds(pl.multiple_of(k * 8 * factor, 8 * factor), 8 * factor)
        for h in range(halves):
            wide[h, at, :] = right_ref[at, h * 128 : (h + 1) * 128].astype(F32)

    @pl.loop(0, factor)
    def _(q):
        part = jnp.concatenate(
            [wide[h, pl.ds(q, seqs, stride=factor), :] for h in range(halves)], axis=1
        ).astype(BF16)
        outer = jnp.dot(left_ref[...], part, preferred_element_type=F32) * (1.0 / seqs)
        at = pl.ds(pl.multiple_of(q * factor, factor), factor)
        stack[:, at, :] = outer.astype(BF16).reshape(rows, factor, cols)

    wl, wlg, wr, wrg = turned(wl_ref), turned(wlg_ref), turned(wr_ref), turned(wrg_ref)
    hidden = wl.shape[0]

    @pl.loop(0, rows)
    def _(i):
        mid = (
            jnp.dot(out_ref[...], stack[i], preferred_element_type=F32)
            + pair_ref[i].astype(F32).T
        ).astype(BF16)
        mid_out[i] = mid
        normed = layer_norm(mid, 0).astype(BF16)
        normed_out[i] = normed

        def project(weight):
            return jnp.dot(weight, normed, preferred_element_type=F32)

        left = sigmoid(project(wlg)) * project(wl)
        right = sigmoid(project(wrg)) * project(wr)
        for h in range(halves):
            lanes = slice(h * 128, (h + 1) * 128)
            left_acc[h, pl.ds(i, hidden, stride=rows), :] = left[:, lanes]
            right_acc[h, pl.ds(i, hidden, stride=rows), :] = right[:, lanes]

    for h in range(halves):
        lanes = slice(h * 128, (h + 1) * 128)
        left_out[:, :, lanes] = left_acc[h].reshape(hidden, rows, 128).astype(BF16)
        right_out[:, :, lanes] = right_acc[h].reshape(hidden, rows, 128).astype(BF16)


def outer_and_gates(left, right, out, pair, wl, wlg, wr, wrg):
    rows, cols, width = pair.shape
    hidden = wl.shape[1]
    depth = right.shape[0]
    factor = left.shape[0] // rows
    chan = jax.ShapeDtypeStruct((hidden, rows, cols), BF16)
    flat = jax.ShapeDtypeStruct((rows, width, cols), BF16)
    return pl.pallas_call(
        functools.partial(outer_kernel, depth // factor),
        out_shape=(chan, chan, flat, flat),
        in_specs=[VMEM] * 8,
        out_specs=(VMEM,) * 4,
        scratch_shapes=[
            pltpu.VMEM((cols // 128, depth, 128), F32),
            pltpu.VMEM((rows, factor * factor, cols), BF16),
            pltpu.VMEM((cols // 128, hidden * rows, 128), F32),
            pltpu.VMEM((cols // 128, hidden * rows, 128), F32),
        ],
        compiler_params=pltpu.CompilerParams(vmem_limit_bytes=48 << 20),
        name="outer_and_gates",
    )(left, right, out, pair, wl, wlg, wr, wrg)


def final_kernel(a_ref, b_ref, mid_ref, normed_ref, gate_ref, out_w_ref, out_ref, wide):
    rows, width, cols = mid_ref.shape
    hidden = a_ref.shape[0]
    for h, ref in enumerate((a_ref, b_ref)):
        wide[h] = ref[...].astype(F32).reshape(hidden * rows, 128)
    gate_w, out_w = turned(gate_ref), turned(out_w_ref)

    @pl.loop(0, rows)
    def _(i):
        product = jnp.concatenate(
            [wide[h, pl.ds(i, hidden, stride=rows), :] for h in range(2)], axis=1
        )
        normed = layer_norm(product, 0).astype(BF16)
        update = jnp.dot(out_w, normed, preferred_element_type=F32)
        gate = sigmoid(jnp.dot(gate_w, normed_ref[i], preferred_element_type=F32))
        out_ref[i] = (mid_ref[i].astype(F32) + gate * update).T.astype(BF16)


def final_update(a, b, mid, normed, gate, out_w):
    rows, width, cols = mid.shape
    hidden = a.shape[0]
    return pl.pallas_call(
        final_kernel,
        out_shape=jax.ShapeDtypeStruct((rows, cols, width), BF16),
        in_specs=[VMEM] * 6,
        out_specs=VMEM,
        scratch_shapes=[pltpu.VMEM((2, hidden * rows, 128), F32)],
        compiler_params=pltpu.CompilerParams(vmem_limit_bytes=32 << 20),
        name="final_update",
    )(a, b, mid, normed, gate, out_w)


def on_device(
    pair,
    alignment,
    opm_left,
    opm_right,
    opm_out,
    tri_left,
    tri_left_gate,
    tri_right,
    tri_right_gate,
    tri_gate,
    tri_out,
):
    rows, cols, width = pair.shape
    factor = opm_left.shape[1]
    hidden = tri_left.shape[1]
    seqs = NZ * NS

    seq_normed = layer_norm(alignment[0], 1).astype(BF16)
    left = jnp.dot(seq_normed, opm_left, preferred_element_type=F32).astype(BF16)
    right = lax.dot_general(
        opm_right, seq_normed, (((0,), (1,)), ((), ())), preferred_element_type=F32
    ).astype(BF16)
    right_all, left_mine = gather_factors(right, left.reshape(2, NS, 2, rows * factor // 2))
    left_rows = left_mine.reshape(seqs, rows * factor).T
    out_w = opm_out.reshape(factor, factor, width).transpose(2, 1, 0).reshape(width, -1)
    left_tri, right_tri, mid, normed = outer_and_gates(
        left_rows,
        right_all.reshape(seqs * factor, cols),
        out_w,
        pair,
        tri_left,
        tri_left_gate,
        tri_right,
        tri_right_gate,
    )
    blocks = (NZ, NS, rows, cols)
    left_all, right_here = spread_triangle(left_tri.reshape(blocks), right_tri.reshape(blocks))
    residues = NZ * NS * rows
    product = jnp.einsum(
        "xik,xjk->ij",
        left_all.reshape(NX, residues, cols),
        right_here.reshape(NX, cols, cols),
        preferred_element_type=F32,
    ).astype(BF16)
    half = (NZ, NS, rows, cols // 2)
    a, b = return_product(
        product[:, : cols // 2].reshape(half), product[:, cols // 2 :].reshape(half)
    )
    chan = (hidden, rows, cols // 2)
    return final_update(a.reshape(chan), b.reshape(chan), mid, normed, tri_gate, tri_out)


def solution(mesh):
    split = P(("row", "seq"), "col", None)
    return jax.shard_map(
        on_device,
        mesh=mesh,
        in_specs=(split, split) + (P(),) * 9,
        out_specs=split,
        check_vma=False,
    )
```

```python
import jax
import jax.numpy as jnp
from jax import lax
from jax.experimental import pallas as pl
from jax.experimental.pallas import tpu as pltpu
from jax.sharding import PartitionSpec as P

EPS = 1e-05
MESH = pl.DeviceIdType.MESH
F32 = jnp.float32
BF16 = jnp.bfloat16
VMEM = pl.BlockSpec(memory_space=pltpu.VMEM)
ANY = pl.BlockSpec(memory_space=pl.ANY)
DMA = pltpu.SemaphoreType.DMA

NX = 4
NZ = 8
NQ = 8
NS = 2 * NQ
NY = NS // 2
HOPS = (1, 7, 2, 6, 3, 5, 4)


class Place:
    def __init__(self):
        row = lax.axis_index("row")
        self.x = lax.axis_index("col")
        seq = lax.axis_index("seq")
        self.z = row // 2
        self.s = (row % 2) * NQ + seq
        self.yy = self.s // 2
        self.core = self.s % 2

    def at(self, z=None, s=None, x=None):
        z = self.z if z is None else z
        s = self.s if s is None else s
        x = self.x if x is None else x
        return (z * 2 + s // NQ, x, s % NQ)


def send(src, dst, send_sem, recv_sem, device):
    pltpu.make_async_remote_copy(
        src_ref=src,
        dst_ref=dst,
        send_sem=send_sem,
        recv_sem=recv_sem,
        device_id=device,
        device_id_type=MESH,
    ).start()


def keep(src, dst, sem):
    pltpu.make_async_copy(src, dst, sem).start()


def await_bytes(ref, sem):
    pltpu.make_async_copy(ref, ref, sem).wait()


def greet(device):
    pl.semaphore_signal(
        pltpu.get_barrier_semaphore(), inc=1, device_id=device, device_id_type=MESH
    )


def layer_norm(values, axis):
    values = values.astype(F32)
    center = values - jnp.mean(values, axis=axis, keepdims=True)
    spread = jnp.mean(center * center, axis=axis, keepdims=True)
    return center * lax.rsqrt(spread + EPS)


def turned(ref):
    return ref[...].astype(F32).T.astype(BF16)


def dot(a, b):
    return jnp.dot(a, b, preferred_element_type=F32)


def lanes(h):
    return slice(h * 128, (h + 1) * 128)


def flat_rows(ref):
    values = ref[...].astype(F32)
    return values.reshape(-1, values.shape[-1]).astype(BF16)


def split_rows(values):
    return values.reshape(-1, 8, values.shape[-1]).astype(BF16)


def factors(align_ref, wl_ref, wr_ref, normed, left_own, right_own):
    cols, width = align_ref.shape[1:]
    p = wl_ref.shape[1]
    seq = layer_norm(align_ref[0], 1).astype(BF16)
    right_own[...] = lax.dot_general(
        turned(wr_ref), seq, (((1,), (1,)), ((), ())), preferred_element_type=F32
    ).astype(BF16)
    wide = seq.astype(F32)
    for h in range(width // 128):
        normed[h] = wide[:, lanes(h)]
    lane = lax.broadcasted_iota(jnp.int32, (p, 8 * p), 1)
    unit = lax.broadcasted_iota(jnp.int32, (p, 8 * p), 0)
    tile = jnp.where(lane % p == unit, 1.0, 0.0).astype(BF16)
    repeated = dot(wl_ref[...], tile)
    group = lax.broadcasted_iota(jnp.int32, repeated.shape, 1) // p
    total = None
    for i in range(8):
        rows = jnp.concatenate(
            [normed[h, pl.ds(i, cols // 8, stride=8), :] for h in range(width // 128)], axis=1
        ).astype(BF16)
        term = dot(rows, jnp.where(group == i, repeated, 0.0).astype(BF16))
        total = term if total is None else total + term
    left_own[...] = total.astype(BF16).reshape(left_own.shape)


def greet_all(me):
    for t in range(1, NS):
        greet(me.at(s=(me.s + t) % NS))
    for t in range(1, NZ):
        greet(me.at(z=(me.z + t) % NZ))
    for t in range(1, NX):
        greet(me.at(x=(me.x + t) % NX))
    owner = me.z // 2
    for t in range(NZ):

        @pl.when(jnp.logical_not(jnp.logical_and(owner == me.x, me.z == t)))
        def _():
            greet(me.at(z=t, x=owner))

    return NS - 1 + NZ - 1 + NX - 1 + 8 - jnp.where(owner == me.x, 1, 0)


def gather(me, left_own, right_own, half, half_wide, mine_send, mine, every, wide, prepare, sems):
    send_sem, first_sem, next_sem, twin_sem, left_sem = sems
    z, s, x, yy, core = me.z, me.s, me.x, me.yy, me.core
    q = right_own.shape[0]
    here = jnp.where(z // 2 == x, 1, 0)

    own = every.at[z, yy, core]
    keep(right_own, own, first_sem)

    @pl.when(core == 0)
    def _():
        for t in HOPS:
            send(right_own, own, send_sem.at[1], first_sem, me.at(z=(z + t) % NZ))

    @pl.when(core == 1)
    def _():
        for t in HOPS:
            send(right_own, own, send_sem.at[1], first_sem, me.at(s=(s + 2 * t) % NS))

    for h in range(2):
        for xt in range(NX):
            zt = 2 * x + h
            same = jnp.logical_and(x == xt, z == zt)

            @pl.when(same)
            def _():
                keep(left_own.at[h], half.at[z], left_sem.at[0])

            @pl.when(jnp.logical_not(same))
            def _():
                send(left_own.at[h], half.at[z], send_sem.at[0], left_sem.at[0], me.at(z=zt, x=xt))

    await_bytes(every.at[:, 0, 0], first_sem)
    twin = me.at(s=s + 1 - 2 * core)

    @pl.when(core == 0)
    def _():
        line = every.at[:, yy, 0]
        for t in HOPS:
            send(line, line, send_sem.at[3], next_sem.at[yy], me.at(s=(s + 2 * t) % NS))
        send(line, line, send_sem.at[4], twin_sem.at[yy], twin)

    @pl.when(core == 1)
    def _():
        line = every.at[z, :, 1]
        for t in HOPS:
            send(line, line, send_sem.at[3], next_sem.at[z], me.at(z=(z + t) % NZ))
        send(line, line, send_sem.at[4], twin_sem.at[z], twin)

    await_bytes(half, left_sem.at[0])
    for h in range(2):
        half_wide[h] = half[:, :, lanes(h)].astype(F32).reshape(NZ * NS, 128)
    for b in range(NS):
        mine_send[b] = jnp.concatenate(
            [half_wide[h, pl.ds(b, NZ, stride=NS), :] for h in range(2)], axis=1
        ).astype(BF16)
    prepare()
    keep(mine_send.at[s], mine.at[s], left_sem.at[1])
    for t in range(1, NS):
        st = (s + t) % NS
        send(mine_send.at[st], mine.at[s], send_sem.at[2], left_sem.at[1], me.at(s=st))

    @pl.when(core == 0)
    def _():
        for t in HOPS:
            yt = (yy + t) % NY
            part = every.at[:, yt, 0]
            await_bytes(part, next_sem.at[yt])
            send(part, part, send_sem.at[4], twin_sem.at[yt], twin)

    @pl.when(core == 1)
    def _():
        for t in HOPS:
            zt = (z + t) % NZ
            part = every.at[zt, :, 1]
            await_bytes(part, next_sem.at[zt])
            send(part, part, send_sem.at[4], twin_sem.at[zt], twin)

    await_bytes(mine, left_sem.at[1])
    for t in range(8):
        await_bytes(every.at[:, 0, 0], twin_sem.at[t])

    @pl.loop(0, NZ * NY)
    def _(k):
        at = pl.ds(pl.multiple_of(k * 2 * q, 2 * q), 2 * q)
        block = every[k // NY, k % NY].astype(F32).reshape(2 * q, -1)
        for h in range(2):
            wide[h, at, :] = block[:, lanes(h)]

    @pl.when(here == 1)
    def _():
        await_bytes(half.at[pl.ds(0, 7)], send_sem.at[0])

    @pl.when(here == 0)
    def _():
        await_bytes(half, send_sem.at[0])

    await_bytes(every.at[pl.ds(0, 7), 0, 0], send_sem.at[1])
    await_bytes(mine.at[pl.ds(0, NS - 1)], send_sem.at[2])
    await_bytes(every.at[pl.ds(0, 7), :, 0], send_sem.at[3])
    await_bytes(every.at[:, :, 0], send_sem.at[4])


def outer_and_gates(mine, mine_wide, wide, out_w, pair, weights, stack, mid_all, normed_all, acc, sides):
    rows, cols, width = pair.shape
    factor = mine.shape[2] // rows
    seqs = NZ * NS
    for h in range(2):
        mine_wide[h] = mine[:, :, lanes(h)].astype(F32).reshape(seqs, 128)
    left = jnp.concatenate(
        [
            jnp.concatenate(
                [mine_wide[h, pl.ds(z, NS, stride=NZ), :] for z in range(NZ)], axis=0
            ).T
            for h in range(2)
        ],
        axis=0,
    ).astype(BF16)

    @pl.loop(0, factor)
    def _(q):
        part = jnp.concatenate(
            [wide[h, pl.ds(q, seqs, stride=factor), :] for h in range(2)], axis=1
        ).astype(BF16)
        outer = dot(left, part) * (1.0 / seqs)
        at = pl.ds(pl.multiple_of(q * factor, factor), factor)
        stack[:, at, :] = outer.astype(BF16).reshape(rows, factor, cols)

    wl, wlg, wr, wrg = (turned(ref) for ref in weights)
    hidden = wl.shape[0]

    @pl.loop(0, rows)
    def _(i):
        mid = (dot(out_w[...], stack[i]) + pair[i].astype(F32).T).astype(BF16)
        mid_all[i] = mid
        normed = layer_norm(mid, 0).astype(BF16)
        normed_all[i] = normed
        for k, (gate, value) in enumerate(((wlg, wl), (wrg, wr))):
            side = jax.nn.sigmoid(dot(gate, normed)) * dot(value, normed)
            for h in range(2):
                acc[k, h, pl.ds(i, hidden, stride=rows), :] = side[:, lanes(h)]

    for k in range(2):
        for h in range(2):
            sides[k][:, :, :, lanes(h)] = split_rows(acc[k, h]).reshape(NZ, NS, rows, 128)


def first_legs(me, a_in, b_in, a_mid, b_mid, send_sem, a_sem, b_sem):
    z, s = me.z, me.s
    keep(a_in.at[:, s], a_mid.at[s], a_sem)
    keep(b_in.at[z], b_mid.at[z], b_sem)
    for t in range(1, NS):
        st = (s + t) % NS
        send(a_in.at[:, st], a_mid.at[s], send_sem.at[0], a_sem, me.at(s=st))
        if t <= len(HOPS):
            zt = (z + HOPS[t - 1]) % NZ
            send(b_in.at[zt], b_mid.at[z], send_sem.at[1], b_sem, me.at(z=zt))


def sent_legs(a_mid, b_mid, send_sem):
    await_bytes(a_mid.at[pl.ds(0, NS - 1)], send_sem.at[0])
    await_bytes(b_mid.at[pl.ds(0, NZ - 1)], send_sem.at[1])
    await_bytes(a_mid.at[:, pl.ds(0, NZ - 1)], send_sem.at[2])
    await_bytes(b_mid.at[:, pl.ds(0, NS - 1)], send_sem.at[3])


def spread(me, a_in, b_in, a_out, b_out, a_mid, b_mid, b_all, sems):
    send_sem, first_sem, a_sem, b_sem, right_sem, left_sem, far_sem, side_sem = sems
    z, s, x = me.z, me.s, me.x
    first_legs(me, a_in, b_in, a_mid, b_mid, send_sem, first_sem.at[0], first_sem.at[1])
    await_bytes(a_mid, first_sem.at[0])
    keep(a_mid.at[:, z], a_out.at[x, z], a_sem.at[z])
    for t in HOPS:
        zt = (z + t) % NZ
        send(a_mid.at[:, zt], a_out.at[x, z], send_sem.at[2], a_sem.at[z], me.at(z=zt))
    await_bytes(b_mid, first_sem.at[1])
    keep(b_mid.at[:, s], b_all.at[:, s], b_sem)
    for t in range(1, NS):
        st = (s + t) % NS
        send(b_mid.at[:, st], b_all.at[:, s], send_sem.at[3], b_sem, me.at(s=st))

    after, before = (x + 1) % NX, (x + 3) % NX

    def pass_on(t):
        zt = (z + t) % NZ
        if t in (0, 5, 6, 7):
            part = a_out.at[before, zt]
            await_bytes(part, left_sem.at[zt])
            send(part, part, send_sem.at[5], far_sem.at[zt], me.at(x=after))
        else:
            part = a_out.at[after, zt]
            await_bytes(part, right_sem.at[zt])
            send(part, part, send_sem.at[5], far_sem.at[zt], me.at(x=before))

    order = (0,) + HOPS
    for k, t in enumerate(order):
        zt = (z + t) % NZ
        part = a_out.at[x, zt]
        await_bytes(part, a_sem.at[zt])
        send(part, part, send_sem.at[4], left_sem.at[zt], me.at(x=after))
        send(part, part, send_sem.at[4], right_sem.at[zt], me.at(x=before))
        if k >= 2:
            pass_on(order[k - 2])
    await_bytes(b_all, b_sem)
    keep(b_all.at[pl.ds(2 * x, 2)], b_out.at[x], side_sem)
    for t in range(1, NX):
        xt = (x + t) % NX
        send(b_all.at[pl.ds(2 * xt, 2)], b_out.at[x], send_sem.at[6], side_sem, me.at(x=xt))
    for t in order[-2:]:
        pass_on(t)
    await_bytes(b_out, side_sem)


def multiply(me, a_out, b_out, product, cols_all, sems):
    right_sem, left_sem, far_sem = sems
    order = (0,) + HOPS
    rows = b_out.shape[1] * b_out.shape[2] * b_out.shape[3]
    for k in range(NX):
        cols_all[k] = flat_rows(b_out.at[k])
    for t in order:
        zt = (me.z + t) % NZ
        part = a_out.at[me.x, zt]
        await_bytes(part, far_sem.at[zt])
        await_bytes(part, (right_sem if t in (0, 5, 6, 7) else left_sem).at[zt])
        total = None
        for k in range(NX):
            term = lax.dot_general(
                flat_rows(a_out.at[k, zt]),
                cols_all[k],
                (((1,), (1,)), ((), ())),
                preferred_element_type=F32,
            )
            total = term if total is None else total + term
        for h in range(2):
            product[h][zt] = split_rows(total[:, lanes(h)])


def bring_back(me, a_in, b_in, a_out, b_out, a_mid, b_mid, sems):
    send_sem, first_sem, last_sem = sems
    z, s = me.z, me.s
    first_legs(me, a_in, b_in, a_mid, b_mid, send_sem, first_sem.at[0], first_sem.at[1])
    await_bytes(a_mid, first_sem.at[0])
    keep(a_mid.at[:, z], a_out.at[z], last_sem.at[0])
    for t in HOPS:
        zt = (z + t) % NZ
        send(a_mid.at[:, zt], a_out.at[z], send_sem.at[2], last_sem.at[0], me.at(z=zt))
    await_bytes(b_mid, first_sem.at[1])
    keep(b_mid.at[:, s], b_out.at[:, s], last_sem.at[1])
    for t in range(1, NS):
        st = (s + t) % NS
        send(b_mid.at[:, st], b_out.at[:, s], send_sem.at[3], last_sem.at[1], me.at(s=st))
    await_bytes(a_out, last_sem.at[0])
    await_bytes(b_out, last_sem.at[1])


def finish(parts, wide, mid_all, normed_all, gate_ref, out_ref, result):
    rows, width, cols = mid_all.shape
    for h, ref in enumerate(parts):
        wide[h] = ref[...].astype(F32).reshape(-1, 128)
    hidden = wide.shape[1] // rows
    gate_w, out_w = turned(gate_ref), turned(out_ref)

    @pl.loop(0, rows)
    def _(i):
        product = jnp.concatenate(
            [wide[h, pl.ds(i, hidden, stride=rows), :] for h in range(2)], axis=1
        )
        normed = layer_norm(product, 0).astype(BF16)
        gate = jax.nn.sigmoid(dot(gate_w, normed_all[i]))
        result[i] = (mid_all[i].astype(F32) + gate * dot(out_w, normed)).T.astype(BF16)


def kernel(
    pair_hbm,
    opm_out_hbm,
    align_ref,
    opm_left_ref,
    opm_right_ref,
    tri_left_ref,
    tri_left_gate_ref,
    tri_right_ref,
    tri_right_gate_ref,
    tri_gate_ref,
    tri_out_ref,
    result,
    pair,
    opm_out,
    opm_wide,
    out_w,
    normed_seq,
    left_own,
    right_own,
    half,
    half_wide,
    mine_send,
    mine,
    every,
    wide,
    stack,
    mid_all,
    normed_all,
    acc,
    left_side,
    right_side,
    a_mid,
    b_mid,
    b_all,
    a_out,
    b_out,
    cols_all,
    product_a,
    product_b,
    pa_mid,
    pb_mid,
    pa_out,
    pb_out,
    load_sem,
    g_send,
    g_first,
    g_next,
    g_twin,
    g_left,
    s_send,
    s_first,
    s_a,
    s_b,
    s_right,
    s_left,
    s_far,
    s_side,
    r_send,
    r_first,
    r_last,
):
    me = Place()
    count = greet_all(me)
    keep(pair_hbm, pair, load_sem.at[0])
    keep(opm_out_hbm, opm_out, load_sem.at[1])
    factors(align_ref, opm_left_ref, opm_right_ref, normed_seq, left_own, right_own)
    pl.semaphore_wait(pltpu.get_barrier_semaphore(), count)

    def prepare():
        await_bytes(opm_out, load_sem.at[1])
        await_bytes(pair, load_sem.at[0])
        opm_wide[...] = opm_out[...].astype(F32)
        p = opm_left_ref.shape[1]
        q = opm_right_ref.shape[1]
        for k in range(q):
            rows = opm_wide[pl.ds(k, p, stride=q), :]
            mine_rows = slice(k * p, (k + 1) * p)
            stack[0, mine_rows, 0:128] = rows.astype(BF16)
        out_w[...] = stack[0, :, 0:128].astype(F32).T.astype(BF16)

    gather(
        me,
        left_own,
        right_own,
        half,
        half_wide,
        mine_send,
        mine,
        every,
        wide,
        prepare,
        (g_send, g_first, g_next, g_twin, g_left),
    )
    outer_and_gates(
        mine,
        half_wide,
        wide,
        out_w,
        pair,
        (tri_left_ref, tri_left_gate_ref, tri_right_ref, tri_right_gate_ref),
        stack,
        mid_all,
        normed_all,
        acc,
        (left_side, right_side),
    )
    spread(
        me,
        left_side,
        right_side,
        a_out,
        b_out,
        a_mid,
        b_mid,
        b_all,
        (s_send, s_first, s_a, s_b, s_right, s_left, s_far, s_side),
    )
    multiply(me, a_out, b_out, (product_a, product_b), cols_all, (s_right, s_left, s_far))
    bring_back(
        me, product_a, product_b, pa_out, pb_out, pa_mid, pb_mid, (r_send, r_first, r_last)
    )
    finish((pa_out, pb_out), acc.at[0], mid_all, normed_all, tri_gate_ref, tri_out_ref, result)

    sent_legs(a_mid, b_mid, s_send)
    await_bytes(a_out.at[pl.ds(0, 2)], s_send.at[4])
    await_bytes(a_out.at[0], s_send.at[5])
    await_bytes(b_out.at[pl.ds(0, NX - 1)], s_send.at[6])
    sent_legs(pa_mid, pb_mid, r_send)


def on_device(pair, alignment, opm_left, opm_right, opm_out, *weights):
    rows, cols, width = pair.shape
    model = alignment.shape[2]
    factor = opm_left.shape[1]
    hidden = weights[0].shape[1]
    seqs = NZ * NS

    def vb(*shape):
        return pltpu.VMEM(shape, BF16)

    def vf(*shape):
        return pltpu.VMEM(shape, F32)

    scratch = [
        vb(rows, cols, width),
        vb(factor * factor, width),
        vf(factor * factor, width),
        vb(width, factor * factor),
        vf(model // 128, cols, 128),
        vb(2, NS, rows * factor),
        vb(factor, cols),
        vb(NZ, NS, rows * factor),
        vf(2, seqs, 128),
        vb(NS, NZ, rows * factor),
        vb(NS, NZ, rows * factor),
        vb(NZ, NY, 2, factor, cols),
        vf(2, seqs * factor, 128),
        vb(rows, factor * factor, cols),
        vb(rows, width, cols),
        vb(rows, width, cols),
        vf(2, 2, hidden * rows, 128),
        vb(NZ, NS, rows, cols),
        vb(NZ, NS, rows, cols),
        vb(NS, NZ, rows, cols),
        vb(NZ, NS, rows, cols),
        vb(NZ, NS, rows, cols),
        vb(NX, NZ, NS, rows, cols),
        vb(NX, NZ // NX, NS, rows, cols),
        vb(NX, cols, cols),
        vb(NZ, NS, rows, 128),
        vb(NZ, NS, rows, 128),
        vb(NS, NZ, rows, 128),
        vb(NZ, NS, rows, 128),
        vb(NZ, NS, rows, 128),
        vb(NZ, NS, rows, 128),
        DMA((2,)),
        DMA((5,)),
        DMA,
        DMA((8,)),
        DMA((8,)),
        DMA((2,)),
        DMA((7,)),
        DMA((2,)),
        DMA((NZ,)),
        DMA,
        DMA((NZ,)),
        DMA((NZ,)),
        DMA((NZ,)),
        DMA,
        DMA((4,)),
        DMA((2,)),
        DMA((2,)),
    ]
    return pl.pallas_call(
        kernel,
        out_shape=jax.ShapeDtypeStruct((rows, cols, width), BF16),
        in_specs=[ANY, ANY] + [VMEM] * 9,
        out_specs=VMEM,
        scratch_shapes=scratch,
        compiler_params=pltpu.CompilerParams(
            collective_id=0, has_side_effects=True, vmem_limit_bytes=56 << 20
        ),
        name="evoformer_pair",
    )(pair, opm_out, alignment, opm_left, opm_right, *weights)


def solution(mesh):
    split = P(("row", "seq"), "col", None)
    return jax.shard_map(
        on_device,
        mesh=mesh,
        in_specs=(split, split) + (P(),) * 9,
        out_specs=split,
        check_vma=False,
    )
```

```python
import jax
import jax.numpy as jnp
from jax import lax
from jax.experimental import pallas as pl
from jax.experimental.pallas import tpu as pltpu
from jax.sharding import PartitionSpec as P

EPS = 1e-05
MESH = pl.DeviceIdType.MESH
F32 = jnp.float32
BF16 = jnp.bfloat16
VMEM = pl.BlockSpec(memory_space=pltpu.VMEM)
ANY = pl.BlockSpec(memory_space=pl.ANY)
DMA = pltpu.SemaphoreType.DMA

NX = 4
NZ = 8
NQ = 8
NS = 2 * NQ
NY = NS // 2
HOPS = (1, 7, 2, 6, 3, 5, 4)


class Place:
    def __init__(self):
        row = lax.axis_index("row")
        self.x = lax.axis_index("col")
        seq = lax.axis_index("seq")
        self.z = row // 2
        self.s = (row % 2) * NQ + seq
        self.yy = self.s // 2
        self.core = self.s % 2

    def at(self, z=None, s=None, x=None):
        z = self.z if z is None else z
        s = self.s if s is None else s
        x = self.x if x is None else x
        return (z * 2 + s // NQ, x, s % NQ)


def send(src, dst, send_sem, recv_sem, device):
    pltpu.make_async_remote_copy(
        src_ref=src,
        dst_ref=dst,
        send_sem=send_sem,
        recv_sem=recv_sem,
        device_id=device,
        device_id_type=MESH,
    ).start()


def keep(src, dst, sem):
    pltpu.make_async_copy(src, dst, sem).start()


def await_bytes(ref, sem):
    pltpu.make_async_copy(ref, ref, sem).wait()


def greet(device):
    pl.semaphore_signal(
        pltpu.get_barrier_semaphore(), inc=1, device_id=device, device_id_type=MESH
    )


def layer_norm(values, axis):
    values = values.astype(F32)
    center = values - jnp.mean(values, axis=axis, keepdims=True)
    spread = jnp.mean(center * center, axis=axis, keepdims=True)
    return center * lax.rsqrt(spread + EPS)


def turned(ref):
    return ref[...].astype(F32).T.astype(BF16)


def dot(a, b):
    return jnp.dot(a, b, preferred_element_type=F32)


def lanes(h):
    return slice(h * 128, (h + 1) * 128)


def flat_rows(ref):
    values = ref[...].astype(F32)
    return values.reshape(-1, values.shape[-1]).astype(BF16)


def split_rows(values):
    return values.reshape(-1, 8, values.shape[-1]).astype(BF16)


def factors(align_ref, wl_ref, wr_ref, normed, left_own, right_own):
    cols, width = align_ref.shape[1:]
    p = wl_ref.shape[0]
    seq = layer_norm(align_ref[0], 1).astype(BF16)
    right_own[...] = lax.dot_general(
        wr_ref[...], seq, (((1,), (1,)), ((), ())), preferred_element_type=F32
    ).astype(BF16)
    wide = seq.astype(F32)
    for h in range(width // 128):
        normed[h] = wide[:, lanes(h)]
    lane = lax.broadcasted_iota(jnp.int32, (p, 8 * p), 1)
    unit = lax.broadcasted_iota(jnp.int32, (p, 8 * p), 0)
    tile = jnp.where(lane % p == unit, 1.0, 0.0).astype(BF16)
    repeated = dot(turned(wl_ref), tile)
    group = lax.broadcasted_iota(jnp.int32, repeated.shape, 1) // p
    total = None
    for i in range(8):
        rows = jnp.concatenate(
            [normed[h, pl.ds(i, cols // 8, stride=8), :] for h in range(width // 128)], axis=1
        ).astype(BF16)
        term = dot(rows, jnp.where(group == i, repeated, 0.0).astype(BF16))
        total = term if total is None else total + term
    left_own[...] = total.astype(BF16).reshape(left_own.shape)


def greet_all(me):
    for t in range(1, NS):
        greet(me.at(s=(me.s + t) % NS))
    for t in range(1, NZ):
        greet(me.at(z=(me.z + t) % NZ))
    for t in range(1, NX):
        greet(me.at(x=(me.x + t) % NX))
    owner = me.z // 2
    for t in range(NZ):

        @pl.when(jnp.logical_not(jnp.logical_and(owner == me.x, me.z == t)))
        def _():
            greet(me.at(z=t, x=owner))

    return NS - 1 + NZ - 1 + NX - 1 + 8 - jnp.where(owner == me.x, 1, 0)


def gather(me, left_own, right_own, half, half_wide, mine_send, mine, every, wide, prepare, sems):
    send_sem, first_sem, next_sem, twin_sem, left_sem = sems
    z, s, x, yy, core = me.z, me.s, me.x, me.yy, me.core
    q = right_own.shape[0]
    here = jnp.where(z // 2 == x, 1, 0)

    own = every.at[z, yy, core]
    keep(right_own, own, first_sem)

    @pl.when(core == 0)
    def _():
        for t in HOPS:
            send(right_own, own, send_sem.at[1], first_sem, me.at(z=(z + t) % NZ))

    @pl.when(core == 1)
    def _():
        for t in HOPS:
            send(right_own, own, send_sem.at[1], first_sem, me.at(s=(s + 2 * t) % NS))

    for h in range(2):
        for xt in range(NX):
            zt = 2 * x + h
            same = jnp.logical_and(x == xt, z == zt)

            @pl.when(same)
            def _():
                keep(left_own.at[h], half.at[z], left_sem.at[0])

            @pl.when(jnp.logical_not(same))
            def _():
                send(left_own.at[h], half.at[z], send_sem.at[0], left_sem.at[0], me.at(z=zt, x=xt))

    await_bytes(every.at[:, 0, 0], first_sem)
    twin = me.at(s=s + 1 - 2 * core)

    @pl.when(core == 0)
    def _():
        line = every.at[:, yy, 0]
        for t in HOPS:
            send(line, line, send_sem.at[3], next_sem.at[yy], me.at(s=(s + 2 * t) % NS))
        send(line, line, send_sem.at[4], twin_sem.at[yy], twin)

    @pl.when(core == 1)
    def _():
        line = every.at[z, :, 1]
        for t in HOPS:
            send(line, line, send_sem.at[3], next_sem.at[z], me.at(z=(z + t) % NZ))
        send(line, line, send_sem.at[4], twin_sem.at[z], twin)

    await_bytes(half, left_sem.at[0])
    for h in range(2):
        half_wide[h] = half[:, :, lanes(h)].astype(F32).reshape(NZ * NS, 128)
    for b in range(NS):
        mine_send[b] = jnp.concatenate(
            [half_wide[h, pl.ds(b, NZ, stride=NS), :] for h in range(2)], axis=1
        ).astype(BF16)
    prepare()
    keep(mine_send.at[s], mine.at[s], left_sem.at[1])
    for t in range(1, NS):
        st = (s + t) % NS
        send(mine_send.at[st], mine.at[s], send_sem.at[2], left_sem.at[1], me.at(s=st))

    @pl.when(core == 0)
    def _():
        for t in HOPS:
            yt = (yy + t) % NY
            part = every.at[:, yt, 0]
            await_bytes(part, next_sem.at[yt])
            send(part, part, send_sem.at[4], twin_sem.at[yt], twin)

    @pl.when(core == 1)
    def _():
        for t in HOPS:
            zt = (z + t) % NZ
            part = every.at[zt, :, 1]
            await_bytes(part, next_sem.at[zt])
            send(part, part, send_sem.at[4], twin_sem.at[zt], twin)

    await_bytes(mine, left_sem.at[1])
    for t in range(8):
        await_bytes(every.at[:, 0, 0], twin_sem.at[t])

    @pl.loop(0, NZ * NY)
    def _(k):
        at = pl.ds(pl.multiple_of(k * 2 * q, 2 * q), 2 * q)
        block = every[k // NY, k % NY].astype(F32).reshape(2 * q, -1)
        for h in range(2):
            wide[h, at, :] = block[:, lanes(h)]

    @pl.when(here == 1)
    def _():
        await_bytes(half.at[pl.ds(0, 7)], send_sem.at[0])

    @pl.when(here == 0)
    def _():
        await_bytes(half, send_sem.at[0])

    await_bytes(every.at[pl.ds(0, 7), 0, 0], send_sem.at[1])
    await_bytes(mine.at[pl.ds(0, NS - 1)], send_sem.at[2])
    await_bytes(every.at[pl.ds(0, 7), :, 0], send_sem.at[3])
    await_bytes(every.at[:, :, 0], send_sem.at[4])


def outer_sums(mine, mine_wide, wide, stack):
    rows, factor, cols = stack.shape[0], mine.shape[2] // stack.shape[0], stack.shape[2]
    seqs = NZ * NS
    for h in range(2):
        mine_wide[h] = mine[:, :, lanes(h)].astype(F32).reshape(seqs, 128)
    left = jnp.concatenate(
        [
            jnp.concatenate(
                [mine_wide[h, pl.ds(z, NS, stride=NZ), :] for z in range(NZ)], axis=0
            ).T
            for h in range(2)
        ],
        axis=0,
    ).astype(BF16)

    @pl.loop(0, factor, unroll=4)
    def _(q):
        part = jnp.concatenate(
            [wide[h, pl.ds(q, seqs, stride=factor), :] for h in range(2)], axis=1
        ).astype(BF16)
        outer = dot(left, part) * (1.0 / seqs)
        at = pl.ds(pl.multiple_of(q * factor, factor), factor)
        stack[:, at, :] = outer.astype(BF16).reshape(rows, factor, cols)


def gated(gate, value, normed, acc, i):
    rows = acc.shape[1] // value.shape[0]
    side = jax.nn.sigmoid(dot(gate, normed)) * dot(value, normed)
    for h in range(2):
        acc[h, pl.ds(i, value.shape[0], stride=rows), :] = side[:, lanes(h)]


def put_side(acc, side):
    for h in range(2):
        side[:, :, :, lanes(h)] = split_rows(acc[h]).reshape(side.shape[:3] + (128,))


def right_gates(out_w, pair, gate_ref, value_ref, stack, mid_all, normed_all, acc, side):
    gate, value = turned(gate_ref), turned(value_ref)

    @pl.loop(0, pair.shape[0], unroll=2)
    def _(i):
        mid = (dot(out_w[...], stack[i]) + pair[i].astype(F32).T).astype(BF16)
        mid_all[i] = mid
        normed = layer_norm(mid, 0).astype(BF16)
        normed_all[i] = normed
        gated(gate, value, normed, acc, i)

    put_side(acc, side)


def left_gates(gate_ref, value_ref, normed_all, acc, side):
    gate, value = turned(gate_ref), turned(value_ref)

    @pl.loop(0, normed_all.shape[0], unroll=2)
    def _(i):
        gated(gate, value, normed_all[i], acc, i)

    put_side(acc, side)


def along_y(me, src, dst, send_sem, sem):
    keep(src(me.s), dst, sem)
    for t in range(1, NS):
        st = (me.s + t) % NS
        send(src(st), dst, send_sem, sem, me.at(s=st))


def along_z(me, src, dst, send_sem, sem):
    keep(src(me.z), dst, sem)
    for t in HOPS:
        zt = (me.z + t) % NZ
        send(src(zt), dst, send_sem, sem, me.at(z=zt))


ORDER = (0,) + HOPS
FROM_LEFT = (0, 5, 6, 7)


def spread(me, a_in, b_in, a_out, b_out, a_mid, b_mid, b_all, sems):
    send_sem, first_sem, a_sem, b_sem, right_sem, left_sem, far_sem, side_sem = sems
    z, s, x = me.z, me.s, me.x
    await_bytes(b_mid, first_sem.at[1])
    along_y(me, lambda st: b_mid.at[:, st], b_all.at[:, s], send_sem.at[3], b_sem.at[s])
    await_bytes(a_mid, first_sem.at[0])
    along_z(me, lambda zt: a_mid.at[:, zt], a_out.at[x, z], send_sem.at[2], a_sem.at[z])

    after, before = (x + 1) % NX, (x + 3) % NX

    def pass_on(t):
        zt = (z + t) % NZ
        if t in FROM_LEFT:
            part = a_out.at[before, zt]
            await_bytes(part, left_sem.at[zt])
            send(part, part, send_sem.at[5], far_sem.at[zt], me.at(x=after))
        else:
            part = a_out.at[after, zt]
            await_bytes(part, right_sem.at[zt])
            send(part, part, send_sem.at[5], far_sem.at[zt], me.at(x=before))

    for k, t in enumerate(ORDER):
        for u in (2 * k, 2 * k + 1):
            su = (s + NS - u) % NS
            await_bytes(b_all.at[:, su], b_sem.at[su])
            for d in (1, 3, 2):
                xt = (x + d) % NX
                send(
                    b_all.at[pl.ds(2 * xt, 2), su],
                    b_out.at[x, :, su],
                    send_sem.at[6],
                    side_sem,
                    me.at(x=xt),
                )
        zt = (z + t) % NZ
        part = a_out.at[x, zt]
        await_bytes(part, a_sem.at[zt])
        send(part, part, send_sem.at[4], left_sem.at[zt], me.at(x=after))
        send(part, part, send_sem.at[4], right_sem.at[zt], me.at(x=before))
        if k >= 2:
            pass_on(ORDER[k - 2])
    keep(b_all.at[pl.ds(2 * x, 2)], b_out.at[x], side_sem)
    return pass_on


def multiply_and_return(
    me, pass_on, a_out, b_out, cols_all, product, y_mid, z_mid, final, arrive_sems, sems
):
    right_sem, left_sem, far_sem, side_sem = arrive_sems
    send_sem, y_sem, z_sem, final_sem = sems
    z, s, x = me.z, me.s, me.x

    def first(t):
        zt = (z + t) % NZ
        part = a_out.at[x, zt]
        await_bytes(part, far_sem.at[zt])
        await_bytes(part, (right_sem if t in FROM_LEFT else left_sem).at[zt])
        total = None
        for k in range(NX):
            term = lax.dot_general(
                flat_rows(a_out.at[k, zt]),
                cols_all[k],
                (((1,), (1,)), ((), ())),
                preferred_element_type=F32,
            )
            total = term if total is None else total + term
        product[zt] = split_rows(total)
        if t == 0:
            along_y(me, lambda st: product.at[zt, st], final.at[z, s], send_sem.at[0], final_sem)
        elif t % 2 == 0:
            along_y(
                me, lambda st: product.at[zt, st], y_mid.at[zt, s], send_sem.at[0], y_sem.at[zt]
            )
        else:
            send(product.at[zt], z_mid.at[z], send_sem.at[2], z_sem.at[z], me.at(z=zt))

    def second(t):
        if t == 0:
            return
        if t % 2 == 0:
            zt = (z + t) % NZ
            await_bytes(y_mid.at[zt], y_sem.at[zt])
            send(y_mid.at[zt], final.at[z], send_sem.at[1], final_sem, me.at(z=zt))
        else:
            zf = (z + NZ - t) % NZ
            await_bytes(z_mid.at[zf], z_sem.at[zf])
            along_y(me, lambda st: z_mid.at[zf, st], final.at[zf, s], send_sem.at[3], final_sem)

    pass_on(ORDER[6])
    await_bytes(b_out, side_sem)
    for k in range(NX):
        cols_all[k] = flat_rows(b_out.at[k])
    for k, t in enumerate(ORDER):
        first(t)
        if k == 1:
            pass_on(ORDER[7])
        if k >= 2:
            second(ORDER[k - 2])
    second(ORDER[6])
    second(ORDER[7])
    await_bytes(final, final_sem)


def finish(parts, wide, mid_all, normed_all, gate_ref, out_ref, result):
    rows, width, cols = mid_all.shape
    for h in range(2):
        wide[h] = parts[:, :, :, lanes(h)].astype(F32).reshape(-1, 128)
    hidden = wide.shape[1] // rows
    gate_w, out_w = turned(gate_ref), turned(out_ref)

    @pl.loop(0, rows)
    def _(i):
        product = jnp.concatenate(
            [wide[h, pl.ds(i, hidden, stride=rows), :] for h in range(2)], axis=1
        )
        normed = layer_norm(product, 0).astype(BF16)
        gate = jax.nn.sigmoid(dot(gate_w, normed_all[i]))
        result[i] = (mid_all[i].astype(F32) + gate * dot(out_w, normed)).T.astype(BF16)


def kernel(
    pair_hbm,
    opm_out_hbm,
    align_ref,
    opm_left_ref,
    opm_right_ref,
    tri_left_ref,
    tri_left_gate_ref,
    tri_right_ref,
    tri_right_gate_ref,
    tri_gate_ref,
    tri_out_ref,
    result,
    pair,
    opm_out,
    opm_wide,
    out_w,
    normed_seq,
    left_own,
    right_own,
    half,
    half_wide,
    mine_send,
    mine,
    every,
    wide,
    stack,
    mid_all,
    normed_all,
    acc,
    left_side,
    right_side,
    a_mid,
    b_mid,
    b_all,
    a_out,
    b_out,
    cols_all,
    product,
    y_mid,
    z_mid,
    final,
    load_sem,
    g_send,
    g_first,
    g_next,
    g_twin,
    g_left,
    s_send,
    s_first,
    s_a,
    s_b,
    s_right,
    s_left,
    s_far,
    s_side,
    r_send,
    r_y,
    r_z,
    r_final,
):
    me = Place()
    count = greet_all(me)
    keep(pair_hbm, pair, load_sem.at[0])
    keep(opm_out_hbm, opm_out, load_sem.at[1])
    factors(align_ref, opm_left_ref, opm_right_ref, normed_seq, left_own, right_own)
    pl.semaphore_wait(pltpu.get_barrier_semaphore(), count)

    def prepare():
        await_bytes(opm_out, load_sem.at[1])
        await_bytes(pair, load_sem.at[0])
        opm_wide[...] = opm_out[...].astype(F32)
        p = opm_left_ref.shape[0]
        q = opm_right_ref.shape[0]
        for k in range(q):
            rows = opm_wide[pl.ds(k, p, stride=q), :]
            mine_rows = slice(k * p, (k + 1) * p)
            stack[0, mine_rows, 0:128] = rows.astype(BF16)
        out_w[...] = stack[0, :, 0:128].astype(F32).T.astype(BF16)

    gather(
        me,
        left_own,
        right_own,
        half,
        half_wide,
        mine_send,
        mine,
        every,
        wide,
        prepare,
        (g_send, g_first, g_next, g_twin, g_left),
    )
    outer_sums(mine, half_wide, wide, stack)
    right_gates(
        out_w,
        pair,
        tri_right_gate_ref,
        tri_right_ref,
        stack,
        mid_all,
        normed_all,
        acc.at[1],
        right_side,
    )
    along_z(me, lambda zt: right_side.at[zt], b_mid.at[me.z], s_send.at[1], s_first.at[1])
    left_gates(tri_left_gate_ref, tri_left_ref, normed_all, acc.at[0], left_side)
    along_y(me, lambda st: left_side.at[:, st], a_mid.at[me.s], s_send.at[0], s_first.at[0])
    pass_on = spread(
        me,
        left_side,
        right_side,
        a_out,
        b_out,
        a_mid,
        b_mid,
        b_all,
        (s_send, s_first, s_a, s_b, s_right, s_left, s_far, s_side),
    )
    multiply_and_return(
        me,
        pass_on,
        a_out,
        b_out,
        cols_all,
        product,
        y_mid,
        z_mid,
        final,
        (s_right, s_left, s_far, s_side),
        (r_send, r_y, r_z, r_final),
    )
    finish(final, acc.at[0], mid_all, normed_all, tri_gate_ref, tri_out_ref, result)
    await_bytes(a_mid.at[pl.ds(0, NS - 1)], s_send.at[0])
    await_bytes(b_mid.at[pl.ds(0, NZ - 1)], s_send.at[1])
    await_bytes(a_mid.at[:, pl.ds(0, NZ - 1)], s_send.at[2])
    await_bytes(b_mid.at[:, pl.ds(0, NS - 1)], s_send.at[3])
    await_bytes(a_out.at[pl.ds(0, 2)], s_send.at[4])
    await_bytes(a_out.at[0], s_send.at[5])
    await_bytes(b_out.at[pl.ds(0, NX - 1)], s_send.at[6])
    await_bytes(final.at[pl.ds(0, 4), pl.ds(0, NS - 1)], r_send.at[0])
    await_bytes(final.at[pl.ds(0, 3)], r_send.at[1])
    await_bytes(final.at[pl.ds(0, 4)], r_send.at[2])
    await_bytes(final.at[pl.ds(0, 4), pl.ds(0, NS - 1)], r_send.at[3])


def on_device(pair, alignment, opm_left, opm_right, opm_out, *weights):
    rows, cols, width = pair.shape
    model = alignment.shape[2]
    factor = opm_left.shape[1]
    hidden = weights[0].shape[1]
    seqs = NZ * NS

    def vb(*shape):
        return pltpu.VMEM(shape, BF16)

    def vf(*shape):
        return pltpu.VMEM(shape, F32)

    scratch = [
        vb(rows, cols, width),
        vb(factor * factor, width),
        vf(factor * factor, width),
        vb(width, factor * factor),
        vf(model // 128, cols, 128),
        vb(2, NS, rows * factor),
        vb(factor, cols),
        vb(NZ, NS, rows * factor),
        vf(2, seqs, 128),
        vb(NS, NZ, rows * factor),
        vb(NS, NZ, rows * factor),
        vb(NZ, NY, 2, factor, cols),
        vf(2, seqs * factor, 128),
        vb(rows, factor * factor, cols),
        vb(rows, width, cols),
        vb(rows, width, cols),
        vf(2, 2, hidden * rows, 128),
        vb(NZ, NS, rows, cols),
        vb(NZ, NS, rows, cols),
        vb(NS, NZ, rows, cols),
        vb(NZ, NS, rows, cols),
        vb(NZ, NS, rows, cols),
        vb(NX, NZ, NS, rows, cols),
        vb(NX, NZ // NX, NS, rows, cols),
        vb(NX, cols, cols),
        vb(NZ, NS, rows, cols),
        vb(NZ, NS, rows, cols),
        vb(NZ, NS, rows, cols),
        vb(NZ, NS, rows, cols),
        DMA((2,)),
        DMA((5,)),
        DMA,
        DMA((8,)),
        DMA((8,)),
        DMA((2,)),
        DMA((7,)),
        DMA((2,)),
        DMA((NZ,)),
        DMA((NS,)),
        DMA((NZ,)),
        DMA((NZ,)),
        DMA((NZ,)),
        DMA,
        DMA((4,)),
        DMA((NZ,)),
        DMA((NZ,)),
        DMA,
    ]
    return pl.pallas_call(
        kernel,
        out_shape=jax.ShapeDtypeStruct((rows, cols, width), BF16),
        in_specs=[ANY, ANY] + [VMEM] * 9,
        out_specs=VMEM,
        scratch_shapes=scratch,
        compiler_params=pltpu.CompilerParams(
            collective_id=0, has_side_effects=True, vmem_limit_bytes=56 << 20
        ),
        name="evoformer_pair",
    )(pair, opm_out, alignment, opm_left.T, opm_right.T, *weights)


def solution(mesh):
    split = P(("row", "seq"), "col", None)
    return jax.shard_map(
        on_device,
        mesh=mesh,
        in_specs=(split, split) + (P(),) * 9,
        out_specs=split,
        check_vma=False,
    )
```

```python
import jax
import jax.numpy as jnp
from jax import lax
from jax.experimental import pallas as pl
from jax.experimental.pallas import tpu as pltpu
from jax.sharding import PartitionSpec as P

EPS = 1e-05
MESH = pl.DeviceIdType.MESH
F32 = jnp.float32
BF16 = jnp.bfloat16
VMEM = pl.BlockSpec(memory_space=pltpu.VMEM)
ANY = pl.BlockSpec(memory_space=pl.ANY)
DMA = pltpu.SemaphoreType.DMA

NX = 4
NZ = 8
NQ = 8
NS = 2 * NQ
NY = NS // 2
HOPS = (1, 7, 2, 6, 3, 5, 4)


class Place:
    def __init__(self):
        row = lax.axis_index("row")
        self.x = lax.axis_index("col")
        seq = lax.axis_index("seq")
        self.z = row // 2
        self.s = (row % 2) * NQ + seq
        self.yy = self.s // 2
        self.core = self.s % 2

    def at(self, z=None, s=None, x=None):
        z = self.z if z is None else z
        s = self.s if s is None else s
        x = self.x if x is None else x
        return (z * 2 + s // NQ, x, s % NQ)


def send(src, dst, send_sem, recv_sem, device):
    pltpu.make_async_remote_copy(
        src_ref=src,
        dst_ref=dst,
        send_sem=send_sem,
        recv_sem=recv_sem,
        device_id=device,
        device_id_type=MESH,
    ).start()


def keep(src, dst, sem):
    pltpu.make_async_copy(src, dst, sem).start()


def await_bytes(ref, sem):
    pltpu.make_async_copy(ref, ref, sem).wait()


def greet(device):
    pl.semaphore_signal(
        pltpu.get_barrier_semaphore(), inc=1, device_id=device, device_id_type=MESH
    )


def layer_norm(values, axis):
    values = values.astype(F32)
    center = values - jnp.mean(values, axis=axis, keepdims=True)
    spread = jnp.mean(center * center, axis=axis, keepdims=True)
    return center * lax.rsqrt(spread + EPS)


def turned(ref):
    return ref[...].astype(F32).T.astype(BF16)


def dot(a, b):
    return jnp.dot(a, b, preferred_element_type=F32)


def lanes(h):
    return slice(h * 128, (h + 1) * 128)


def flat_rows(ref):
    values = ref[...].astype(F32)
    return values.reshape(-1, values.shape[-1]).astype(BF16)


def split_rows(values):
    return values.reshape(-1, 8, values.shape[-1]).astype(BF16)


def factors(align_ref, wl_ref, wr_ref, normed, left_own, right_own):
    cols, width = align_ref.shape[1:]
    p = wl_ref.shape[0]
    seq = layer_norm(align_ref[0], 1).astype(BF16)
    right_own[...] = lax.dot_general(
        wr_ref[...], seq, (((1,), (1,)), ((), ())), preferred_element_type=F32
    ).astype(BF16)
    wide = seq.astype(F32)
    for h in range(width // 128):
        normed[h] = wide[:, lanes(h)]
    lane = lax.broadcasted_iota(jnp.int32, (p, 8 * p), 1)
    unit = lax.broadcasted_iota(jnp.int32, (p, 8 * p), 0)
    tile = jnp.where(lane % p == unit, 1.0, 0.0).astype(BF16)
    repeated = dot(turned(wl_ref), tile)
    group = lax.broadcasted_iota(jnp.int32, repeated.shape, 1) // p
    total = None
    for i in range(8):
        rows = jnp.concatenate(
            [normed[h, pl.ds(i, cols // 8, stride=8), :] for h in range(width // 128)], axis=1
        ).astype(BF16)
        term = dot(rows, jnp.where(group == i, repeated, 0.0).astype(BF16))
        total = term if total is None else total + term
    left_own[...] = total.astype(BF16).reshape(left_own.shape)


def greet_all(me):
    for t in range(1, NS):
        greet(me.at(s=(me.s + t) % NS))
    for t in range(1, NZ):
        greet(me.at(z=(me.z + t) % NZ))
    for t in range(1, NX):
        greet(me.at(x=(me.x + t) % NX))
    owner = me.z // 2
    for t in range(NZ):

        @pl.when(jnp.logical_not(jnp.logical_and(owner == me.x, me.z == t)))
        def _():
            greet(me.at(z=t, x=owner))

    return NS - 1 + NZ - 1 + NX - 1 + 8 - jnp.where(owner == me.x, 1, 0)


def gather(me, left_own, right_own, half, half_wide, mine_send, mine, every, wide, sems):
    send_sem, first_sem, next_sem, twin_sem, left_sem = sems
    z, s, x, yy, core = me.z, me.s, me.x, me.yy, me.core
    q = right_own.shape[0]
    here = jnp.where(z // 2 == x, 1, 0)

    own = every.at[z, yy, core]
    keep(right_own, own, first_sem)

    @pl.when(core == 0)
    def _():
        for t in HOPS:
            send(right_own, own, send_sem.at[1], first_sem, me.at(z=(z + t) % NZ))

    @pl.when(core == 1)
    def _():
        for t in HOPS:
            send(right_own, own, send_sem.at[1], first_sem, me.at(s=(s + 2 * t) % NS))

    for h in range(2):
        for xt in range(NX):
            zt = 2 * x + h
            same = jnp.logical_and(x == xt, z == zt)

            @pl.when(same)
            def _():
                keep(left_own.at[h], half.at[z], left_sem.at[0])

            @pl.when(jnp.logical_not(same))
            def _():
                send(left_own.at[h], half.at[z], send_sem.at[0], left_sem.at[0], me.at(z=zt, x=xt))

    await_bytes(every.at[:, 0, 0], first_sem)
    twin = me.at(s=s + 1 - 2 * core)

    def line(c, p, half_line):
        at = pl.ds(4 * half_line, 4)
        return every.at[at, index_of(c, p), 0] if c == 0 else every.at[index_of(c, p), at, 1]

    def index_of(c, p):
        return p % 2 * 4 + p // 2 if c == 0 else p

    def place_of(c):
        return yy % 4 * 2 + yy // 4 if c == 0 else z

    def peer(c, p):
        return me.at(s=2 * index_of(c, p)) if c == 0 else me.at(z=p)

    def widen(c, p, half_line):
        @pl.loop(0, 4)
        def _(j):
            n = (4 * half_line + j) * NS + 2 * index_of(c, p)
            if c == 1:
                n = index_of(c, p) * NS + 2 * (4 * half_line + j) + 1
            at = pl.ds(pl.multiple_of(n * q, q), q)
            block = line(c, p, half_line)[j].astype(F32)
            for h in range(2):
                wide[h, at, :] = block[:, lanes(h)]

    events = [
        (d, way, half_line)
        for d in range(1, 5)
        for half_line in range(2)
        for way in range(2)
        if d <= 3 + (way == half_line)
    ]

    def moved(c, d, way):
        return (place_of(c) + (NZ - d if way == 0 else d)) % NZ

    for c in range(2):

        @pl.when(core == c)
        def _(c=c):
            here_p = place_of(c)
            ends = ((here_p + 1) % NZ, (here_p + NZ - 1) % NZ)
            for half_line in range(2):
                part = line(c, here_p, half_line)
                for end in ends:
                    send(
                        part,
                        part,
                        send_sem.at[3],
                        next_sem.at[index_of(c, here_p), half_line],
                        peer(c, end),
                    )
                send(
                    part,
                    part,
                    send_sem.at[4],
                    twin_sem.at[index_of(c, here_p), half_line],
                    twin,
                )

    await_bytes(half, left_sem.at[0])
    for h in range(2):
        half_wide[h] = half[:, :, lanes(h)].astype(F32).reshape(NZ * NS, 128)
    for b in range(NS):
        mine_send[b] = jnp.concatenate(
            [half_wide[h, pl.ds(b, NZ, stride=NS), :] for h in range(2)], axis=1
        ).astype(BF16)
    keep(mine_send.at[s], mine.at[s], left_sem.at[1])
    for t in range(1, NS):
        st = (s + t) % NS
        send(mine_send.at[st], mine.at[s], send_sem.at[2], left_sem.at[1], me.at(s=st))

    for c in range(2):

        @pl.when(core == c)
        def _(c=c):
            here_p = place_of(c)
            ends = ((here_p + 1) % NZ, (here_p + NZ - 1) % NZ)
            steps = [(here_p, 0, 0, 0), (here_p, 0, 0, 1)] + [
                (moved(c, d, way), d, way, half_line) for d, way, half_line in events
            ]
            far_p = place_of(1 - c)
            far_steps = [(far_p, 0), (far_p, 1)] + [
                (moved(1 - c, d, way), half_line) for d, way, half_line in events
            ]

            def from_twin(k):
                p, half_line = far_steps[k]
                part = line(1 - c, p, half_line)
                await_bytes(part, twin_sem.at[index_of(1 - c, p), half_line])
                widen(1 - c, p, half_line)

            for k, (p, d, way, half_line) in enumerate(steps):
                part = line(c, p, half_line)
                if d:
                    sem = next_sem.at[index_of(c, p), half_line]
                    await_bytes(part, sem)
                    if d < 3 + (way == half_line):
                        send(part, part, send_sem.at[3], sem, peer(c, ends[way]))
                    send(
                        part,
                        part,
                        send_sem.at[4],
                        twin_sem.at[index_of(c, p), half_line],
                        twin,
                    )
                widen(c, p, half_line)
                if k >= 4:
                    from_twin(k - 4)
            for k in range(len(steps) - 4, len(steps)):
                from_twin(k)

    await_bytes(mine, left_sem.at[1])

    @pl.when(here == 1)
    def _():
        await_bytes(half.at[pl.ds(0, 7)], send_sem.at[0])

    @pl.when(here == 0)
    def _():
        await_bytes(half, send_sem.at[0])

    await_bytes(every.at[pl.ds(0, 7), 0, 0], send_sem.at[1])
    await_bytes(mine.at[pl.ds(0, NS - 1)], send_sem.at[2])
    await_bytes(every.at[pl.ds(0, 7), :, 0], send_sem.at[3])
    await_bytes(every.at[:, :, 0], send_sem.at[4])


def outer_sums(mine, mine_wide, wide, stack):
    rows, factor, cols = stack.shape[0], mine.shape[2] // stack.shape[0], stack.shape[2]
    seqs = NZ * NS
    for h in range(2):
        mine_wide[h] = mine[:, :, lanes(h)].astype(F32).reshape(seqs, 128)
    left = jnp.concatenate(
        [
            jnp.concatenate(
                [mine_wide[h, pl.ds(z, NS, stride=NZ), :] for z in range(NZ)], axis=0
            ).T
            for h in range(2)
        ],
        axis=0,
    ).astype(BF16)

    @pl.loop(0, factor, unroll=4)
    def _(q):
        part = jnp.concatenate(
            [wide[h, pl.ds(q, seqs, stride=factor), :] for h in range(2)], axis=1
        ).astype(BF16)
        outer = dot(left, part) * (1.0 / seqs)
        at = pl.ds(pl.multiple_of(q * factor, factor), factor)
        stack[:, at, :] = outer.astype(BF16).reshape(rows, factor, cols)


def gated(gate, value, normed, acc, i):
    rows = acc.shape[1] // value.shape[0]
    side = jax.nn.sigmoid(dot(gate, normed)) * dot(value, normed)
    for h in range(2):
        acc[h, pl.ds(i, value.shape[0], stride=rows), :] = side[:, lanes(h)]


def put_side(acc, side):
    for h in range(2):
        side[h] = split_rows(acc[h]).reshape(side.shape[1:])


def left_gates(out_w, pair, gate_ref, value_ref, stack, mid_all, normed_all, acc, side):
    gate, value = turned(gate_ref), turned(value_ref)

    @pl.loop(0, pair.shape[0], unroll=2)
    def _(i):
        mid = (dot(out_w[...], stack[i]) + pair[i].astype(F32).T).astype(BF16)
        mid_all[i] = mid
        normed = layer_norm(mid, 0).astype(BF16)
        normed_all[i] = normed
        gated(gate, value, normed, acc, i)

    put_side(acc, side)


def right_gates(gate_ref, value_ref, normed_all, acc, side):
    gate, value = turned(gate_ref), turned(value_ref)

    @pl.loop(0, normed_all.shape[0], unroll=2)
    def _(i):
        gated(gate, value, normed_all[i], acc, i)

    put_side(acc, side)


def along_y(me, src, dst, send_sem, sem, offsets=range(NS)):
    for t in offsets:
        if t == 0:
            keep(src(me.s), dst, sem)
        else:
            st = (me.s + t) % NS
            send(src(st), dst, send_sem, sem, me.at(s=st))


def along_z(me, src, dst, send_sem, sem, offsets=(0,) + HOPS):
    for t in offsets:
        if t == 0:
            keep(src(me.z), dst, sem)
        else:
            zt = (me.z + t) % NZ
            send(src(zt), dst, send_sem, sem, me.at(z=zt))


ORDER = (0,) + HOPS
UNITS = NZ + NS
LAG = 8


def left_legs(me, side, y_mid, z_mid, out, sems):
    send_sem, first_sem, z_sem, s_sem = sems
    await_bytes(y_mid, first_sem.at[0])
    along_z(me, lambda zt: y_mid.at[:, zt], out.at[0, me.z], send_sem.at[2], z_sem.at[me.z])
    await_bytes(z_mid, first_sem.at[1])
    along_y(me, lambda st: z_mid.at[:, st], out.at[1, :, me.s], send_sem.at[3], s_sem.at[me.s])


def first_legs(me, side, y_mid, z_mid, send_sem, first_sem, parts=(0, 1)):
    for part in parts:
        along_y(
            me,
            lambda st: side.at[0, :, st],
            y_mid.at[me.s],
            send_sem.at[0],
            first_sem.at[0],
            range(part, NS, 2),
        )
        along_z(
            me,
            lambda zt: side.at[1, zt],
            z_mid.at[me.z],
            send_sem.at[1],
            first_sem.at[1],
            ORDER[4 * part : 4 * part + 4],
        )


def legs_left(y_mid, z_mid, send_sem):
    await_bytes(y_mid.at[pl.ds(0, NS - 1)], send_sem.at[0])
    await_bytes(z_mid.at[pl.ds(0, NZ - 1)], send_sem.at[1])
    await_bytes(y_mid.at[:, pl.ds(0, NZ - 1)], send_sem.at[2])
    await_bytes(z_mid.at[:, pl.ds(0, NS - 1)], send_sem.at[3])


def spread(me, left_side, right_side, right_gates, a_out, rows_all, b_all, b_out, mids, l_sems, r_sems, x_sems):
    z, s, x = me.z, me.s, me.x
    ly_mid, lz_mid, ry_mid, rz_mid = mids
    x_send, near_sem, far_sem, side_sem = x_sems
    first_legs(me, left_side, ly_mid, lz_mid, l_sems[0], l_sems[1])
    right_gates()
    first_legs(me, right_side, ry_mid, rz_mid, r_sems[0], r_sems[1], (0,))
    left_legs(me, left_side, ly_mid, lz_mid, a_out.at[:, x], l_sems)
    first_legs(me, right_side, ry_mid, rz_mid, r_sems[0], r_sems[1], (1,))

    after, before = (x + 1) % NX, (x + 3) % NX

    def unit(k):
        if k < NZ:
            zt = (z + ORDER[k]) % NZ
            return zt, lambda xt: a_out.at[0, xt, zt], l_sems[2].at[zt]
        st = (s + 2 * NS - k + NZ) % NS
        return NZ + st, lambda xt: a_out.at[1, xt, :, st], l_sems[3].at[st]

    def pass_on(k):
        n, place, _ = unit(k)
        way = k % 2
        part = place(after if way else before)
        await_bytes(part, near_sem.at[way, n])
        send(part, part, x_send.at[1], far_sem.at[n], me.at(x=before if way else after))

    for k in range(UNITS):
        n, place, sem = unit(k)
        part = place(x)
        await_bytes(part, sem)
        send(part, part, x_send.at[0], near_sem.at[0, n], me.at(x=after))
        send(part, part, x_send.at[0], near_sem.at[1, n], me.at(x=before))
        if k >= LAG:
            pass_on(k - LAG)
        if k == UNITS - 8:
            left_legs(me, right_side, ry_mid, rz_mid, b_all, r_sems)
    for k in range(UNITS - LAG, UNITS):
        pass_on(k)

    for k in range(NZ):
        zt = (z + ORDER[k]) % NZ
        xt = zt // 2
        part, there = b_all.at[0, zt], b_out.at[0, x, zt % 2]
        await_bytes(part, r_sems[2].at[zt])

        @pl.when(xt == x)
        def _():
            keep(part, there, side_sem)

        @pl.when(xt != x)
        def _():
            send(part, there, x_send.at[2], side_sem, me.at(x=xt))

        for u in (2 * k, 2 * k + 1):
            su = (s + NS - u) % NS
            await_bytes(b_all.at[1, :, su], r_sems[3].at[su])
            for d in (1, 3, 2):
                xt = (x + d) % NX
                send(
                    b_all.at[1, pl.ds(2 * xt, 2), su],
                    b_out.at[1, x, :, su],
                    x_send.at[2],
                    side_sem,
                    me.at(x=xt),
                )
    keep(b_all.at[1, pl.ds(2 * x, 2)], b_out.at[1, x], side_sem)

    for k in range(UNITS):
        n, place, _ = unit(k)
        part = place(x)
        await_bytes(part, far_sem.at[n])
        await_bytes(part, near_sem.at[1 - k % 2, n])

    @pl.loop(0, NX * NZ, unroll=2)
    def _(k):
        xt, zt = k // NZ, k % NZ
        for h in range(2):
            rows_all[xt, zt, :, lanes(h)] = flat_rows(a_out.at[h, xt, zt])

    await_bytes(b_out, side_sem)


def multiply_and_return(me, rows_all, b_out, cols_all, product, y_mid, z_mid, final, sems):
    send_sem, first_sem, final_sem = sems
    z, s = me.z, me.s
    for k in range(NX):
        for h in range(2):
            cols_all[k, :, lanes(h)] = flat_rows(b_out.at[h, k])
    for t in ORDER:
        zt = (z + t) % NZ
        total = None
        for k in range(NX):
            term = lax.dot_general(
                rows_all[k, zt], cols_all[k], (((1,), (1,)), ((), ())), preferred_element_type=F32
            )
            total = term if total is None else total + term
        for h in range(2):
            product[h, zt] = split_rows(total[:, lanes(h)])
        if t == 0:
            keep(product.at[1, z], z_mid.at[z], first_sem.at[1])
        else:
            send(product.at[1, zt], z_mid.at[z], send_sem.at[1], first_sem.at[1], me.at(z=zt))
    along_y(me, lambda st: product.at[0, :, st], y_mid.at[s], send_sem.at[0], first_sem.at[0])
    await_bytes(z_mid, first_sem.at[1])
    along_y(me, lambda st: z_mid.at[:, st], final.at[1, :, s], send_sem.at[3], final_sem)
    await_bytes(y_mid, first_sem.at[0])
    along_z(me, lambda zt: y_mid.at[:, zt], final.at[0, z], send_sem.at[2], final_sem)
    await_bytes(final, final_sem)


def finish(parts, wide, mid_all, normed_all, gate_ref, out_ref, result):
    rows, width, cols = mid_all.shape
    for h in range(2):
        wide[h] = parts[h].astype(F32).reshape(-1, 128)
    hidden = wide.shape[1] // rows
    gate_w, out_w = turned(gate_ref), turned(out_ref)

    @pl.loop(0, rows)
    def _(i):
        product = jnp.concatenate(
            [wide[h, pl.ds(i, hidden, stride=rows), :] for h in range(2)], axis=1
        )
        normed = layer_norm(product, 0).astype(BF16)
        gate = jax.nn.sigmoid(dot(gate_w, normed_all[i]))
        result[i] = (mid_all[i].astype(F32) + gate * dot(out_w, normed)).T.astype(BF16)


def kernel(
    pair_hbm,
    opm_out_hbm,
    align_ref,
    opm_left_ref,
    opm_right_ref,
    tri_left_ref,
    tri_left_gate_ref,
    tri_right_ref,
    tri_right_gate_ref,
    tri_gate_ref,
    tri_out_ref,
    result,
    pair,
    opm_out,
    opm_wide,
    out_w,
    normed_seq,
    left_own,
    right_own,
    half,
    half_wide,
    mine_send,
    mine,
    every,
    wide,
    stack,
    mid_all,
    normed_all,
    acc,
    left_side,
    right_side,
    ly_mid,
    lz_mid,
    ry_mid,
    rz_mid,
    py_mid,
    pz_mid,
    b_all,
    a_out,
    rows_all,
    b_out,
    cols_all,
    product,
    final,
    load_sem,
    g_send,
    g_first,
    g_next,
    g_twin,
    g_left,
    l_send,
    l_first,
    l_z,
    l_s,
    r_send,
    r_first,
    r_z,
    r_s,
    x_send,
    x_near,
    x_far,
    x_side,
    p_send,
    p_first,
    p_final,
):
    me = Place()
    count = greet_all(me)
    keep(pair_hbm, pair, load_sem.at[0])
    keep(opm_out_hbm, opm_out, load_sem.at[1])
    factors(align_ref, opm_left_ref, opm_right_ref, normed_seq, left_own, right_own)
    await_bytes(opm_out, load_sem.at[1])
    await_bytes(pair, load_sem.at[0])
    opm_wide[...] = opm_out[...].astype(F32)
    p = opm_left_ref.shape[0]
    q = opm_right_ref.shape[0]
    for k in range(q):
        rows = opm_wide[pl.ds(k, p, stride=q), :]
        mine_rows = slice(k * p, (k + 1) * p)
        stack[0, mine_rows, 0:128] = rows.astype(BF16)
    out_w[...] = stack[0, :, 0:128].astype(F32).T.astype(BF16)
    pl.semaphore_wait(pltpu.get_barrier_semaphore(), count)

    gather(
        me,
        left_own,
        right_own,
        half,
        half_wide,
        mine_send,
        mine,
        every,
        wide,
        (g_send, g_first, g_next, g_twin, g_left),
    )
    outer_sums(mine, half_wide, wide, stack)
    left_gates(
        out_w,
        pair,
        tri_left_gate_ref,
        tri_left_ref,
        stack,
        mid_all,
        normed_all,
        acc.at[0],
        left_side,
    )
    spread(
        me,
        left_side,
        right_side,
        lambda: right_gates(
            tri_right_gate_ref, tri_right_ref, normed_all, acc.at[1], right_side
        ),
        a_out,
        rows_all,
        b_all,
        b_out,
        (ly_mid, lz_mid, ry_mid, rz_mid),
        (l_send, l_first, l_z, l_s),
        (r_send, r_first, r_z, r_s),
        (x_send, x_near, x_far, x_side),
    )
    multiply_and_return(
        me, rows_all, b_out, cols_all, product, py_mid, pz_mid, final, (p_send, p_first, p_final)
    )
    finish(final, acc.at[0], mid_all, normed_all, tri_gate_ref, tri_out_ref, result)
    legs_left(ly_mid, lz_mid, l_send)
    legs_left(ry_mid, rz_mid, r_send)
    await_bytes(a_out.at[:, pl.ds(0, 2)], x_send.at[0])
    await_bytes(a_out.at[:, 0], x_send.at[1])
    await_bytes(b_out.at[:, pl.ds(0, NX - 1)], x_send.at[2])
    legs_left(py_mid, pz_mid, p_send)


def on_device(pair, alignment, opm_left, opm_right, opm_out, *weights):
    rows, cols, width = pair.shape
    model = alignment.shape[2]
    factor = opm_left.shape[1]
    hidden = weights[0].shape[1]
    seqs = NZ * NS

    def vb(*shape):
        return pltpu.VMEM(shape, BF16)

    def vf(*shape):
        return pltpu.VMEM(shape, F32)

    scratch = [
        vb(rows, cols, width),
        vb(factor * factor, width),
        vf(factor * factor, width),
        vb(width, factor * factor),
        vf(model // 128, cols, 128),
        vb(2, NS, rows * factor),
        vb(factor, cols),
        vb(NZ, NS, rows * factor),
        vf(2, seqs, 128),
        vb(NS, NZ, rows * factor),
        vb(NS, NZ, rows * factor),
        vb(NZ, NY, 2, factor, cols),
        vf(2, seqs * factor, 128),
        vb(rows, factor * factor, cols),
        vb(rows, width, cols),
        vb(rows, width, cols),
        vf(2, 2, hidden * rows, 128),
        vb(2, NZ, NS, rows, 128),
        vb(2, NZ, NS, rows, 128),
        vb(NS, NZ, rows, 128),
        vb(NZ, NS, rows, 128),
        vb(NS, NZ, rows, 128),
        vb(NZ, NS, rows, 128),
        vb(NS, NZ, rows, 128),
        vb(NZ, NS, rows, 128),
        vb(2, NZ, NS, rows, 128),
        vb(2, NX, NZ, NS, rows, 128),
        vb(NX, NZ, NS * rows, cols),
        vb(2, NX, NZ // NX, NS, rows, 128),
        vb(NX, cols, cols),
        vb(2, NZ, NS, rows, 128),
        vb(2, NZ, NS, rows, 128),
        DMA((2,)),
        DMA((5,)),
        DMA,
        DMA((8, 2)),
        DMA((8, 2)),
        DMA((2,)),
        DMA((4,)),
        DMA((2,)),
        DMA((NZ,)),
        DMA((NS,)),
        DMA((4,)),
        DMA((2,)),
        DMA((NZ,)),
        DMA((NS,)),
        DMA((3,)),
        DMA((2, UNITS)),
        DMA((UNITS,)),
        DMA,
        DMA((4,)),
        DMA((2,)),
        DMA,
    ]
    return pl.pallas_call(
        kernel,
        out_shape=jax.ShapeDtypeStruct((rows, cols, width), BF16),
        in_specs=[ANY, ANY] + [VMEM] * 9,
        out_specs=VMEM,
        scratch_shapes=scratch,
        compiler_params=pltpu.CompilerParams(
            collective_id=0, has_side_effects=True, vmem_limit_bytes=56 << 20
        ),
        name="evoformer_pair",
    )(pair, opm_out, alignment, opm_left.T, opm_right.T, *weights)


def solution(mesh):
    split = P(("row", "seq"), "col", None)
    return jax.shard_map(
        on_device,
        mesh=mesh,
        in_specs=(split, split) + (P(),) * 9,
        out_specs=split,
        check_vma=False,
    )
```

```python
import jax
import jax.numpy as jnp
from jax import lax
from jax.experimental import pallas as pl
from jax.experimental.pallas import tpu as pltpu
from jax.sharding import PartitionSpec as P

EPS = 1e-05
MESH = pl.DeviceIdType.MESH
F32 = jnp.float32
BF16 = jnp.bfloat16
VMEM = pl.BlockSpec(memory_space=pltpu.VMEM)
ANY = pl.BlockSpec(memory_space=pl.ANY)
DMA = pltpu.SemaphoreType.DMA

NX = 4
NZ = 8
NQ = 8
NS = 2 * NQ
NY = NS // 2
HOPS = (1, 7, 2, 6, 3, 5, 4)


class Place:
    def __init__(self):
        row = lax.axis_index("row")
        self.x = lax.axis_index("col")
        seq = lax.axis_index("seq")
        self.z = row // 2
        self.s = (row % 2) * NQ + seq
        self.yy = self.s // 2
        self.core = self.s % 2

    def at(self, z=None, s=None, x=None):
        z = self.z if z is None else z
        s = self.s if s is None else s
        x = self.x if x is None else x
        return (z * 2 + s // NQ, x, s % NQ)


def send(src, dst, send_sem, recv_sem, device):
    pltpu.make_async_remote_copy(
        src_ref=src,
        dst_ref=dst,
        send_sem=send_sem,
        recv_sem=recv_sem,
        device_id=device,
        device_id_type=MESH,
    ).start()


def keep(src, dst, sem):
    pltpu.make_async_copy(src, dst, sem).start()


def await_bytes(ref, sem):
    pltpu.make_async_copy(ref, ref, sem).wait()


def greet(device):
    pl.semaphore_signal(
        pltpu.get_barrier_semaphore(), inc=1, device_id=device, device_id_type=MESH
    )


def layer_norm(values, axis):
    values = values.astype(F32)
    center = values - jnp.mean(values, axis=axis, keepdims=True)
    spread = jnp.mean(center * center, axis=axis, keepdims=True)
    return center * lax.rsqrt(spread + EPS)


def turned(ref):
    return ref[...].astype(F32).T.astype(BF16)


def dot(a, b):
    return jnp.dot(a, b, preferred_element_type=F32)


def lanes(h):
    return slice(h * 128, (h + 1) * 128)


def flat_rows(ref):
    values = ref[...].astype(F32)
    return values.reshape(-1, values.shape[-1]).astype(BF16)


def split_rows(values):
    return values.reshape(-1, 8, values.shape[-1]).astype(BF16)


def factors(align_ref, wl_ref, wr_ref, normed, left_own, right_own):
    cols, width = align_ref.shape[1:]
    p = wl_ref.shape[0]
    seq = layer_norm(align_ref[0], 1).astype(BF16)
    right_own[...] = lax.dot_general(
        wr_ref[...], seq, (((1,), (1,)), ((), ())), preferred_element_type=F32
    ).astype(BF16)
    wide = seq.astype(F32)
    for h in range(width // 128):
        normed[h] = wide[:, lanes(h)]
    lane = lax.broadcasted_iota(jnp.int32, (p, 8 * p), 1)
    unit = lax.broadcasted_iota(jnp.int32, (p, 8 * p), 0)
    tile = jnp.where(lane % p == unit, 1.0, 0.0).astype(BF16)
    repeated = dot(turned(wl_ref), tile)
    group = lax.broadcasted_iota(jnp.int32, repeated.shape, 1) // p
    total = None
    for i in range(8):
        rows = jnp.concatenate(
            [normed[h, pl.ds(i, cols // 8, stride=8), :] for h in range(width // 128)], axis=1
        ).astype(BF16)
        term = dot(rows, jnp.where(group == i, repeated, 0.0).astype(BF16))
        total = term if total is None else total + term
    left_own[...] = total.astype(BF16).reshape(left_own.shape)


def greet_all(me):
    for t in range(1, NS):
        greet(me.at(s=(me.s + t) % NS))
    for t in range(1, NZ):
        greet(me.at(z=(me.z + t) % NZ))
    for t in range(1, NX):
        greet(me.at(x=(me.x + t) % NX))
    owner = me.z // 2
    for t in range(NZ):

        @pl.when(jnp.logical_not(jnp.logical_and(owner == me.x, me.z == t)))
        def _():
            greet(me.at(z=t, x=owner))

    return NS - 1 + NZ - 1 + NX - 1 + 8 - jnp.where(owner == me.x, 1, 0)


def gather(me, left_own, right_own, half, half_wide, mine_send, mine, every, wide, sems):
    send_sem, first_sem, next_sem, twin_sem, left_sem = sems
    z, s, x, yy, core = me.z, me.s, me.x, me.yy, me.core
    q = right_own.shape[0]
    here = jnp.where(z // 2 == x, 1, 0)

    own = every.at[z, yy, core]
    keep(right_own, own, first_sem)

    @pl.when(core == 0)
    def _():
        for t in HOPS:
            send(right_own, own, send_sem.at[1], first_sem, me.at(z=(z + t) % NZ))

    @pl.when(core == 1)
    def _():
        for t in HOPS:
            send(right_own, own, send_sem.at[1], first_sem, me.at(s=(s + 2 * t) % NS))

    for h in range(2):
        for xt in range(NX):
            zt = 2 * x + h
            same = jnp.logical_and(x == xt, z == zt)

            @pl.when(same)
            def _():
                keep(left_own.at[h], half.at[z], left_sem.at[0])

            @pl.when(jnp.logical_not(same))
            def _():
                send(left_own.at[h], half.at[z], send_sem.at[0], left_sem.at[0], me.at(z=zt, x=xt))

    await_bytes(every.at[:, 0, 0], first_sem)
    twin = me.at(s=s + 1 - 2 * core)

    def line(c, p, half_line):
        at = pl.ds(4 * half_line, 4)
        return every.at[at, index_of(c, p), 0] if c == 0 else every.at[index_of(c, p), at, 1]

    def index_of(c, p):
        return p % 2 * 4 + p // 2 if c == 0 else p

    def place_of(c):
        return yy % 4 * 2 + yy // 4 if c == 0 else z

    def peer(c, p):
        return me.at(s=2 * index_of(c, p)) if c == 0 else me.at(z=p)

    def widen(c, p, half_line):
        @pl.loop(0, 4)
        def _(j):
            n = (4 * half_line + j) * NS + 2 * index_of(c, p)
            if c == 1:
                n = index_of(c, p) * NS + 2 * (4 * half_line + j) + 1
            at = pl.ds(pl.multiple_of(n * q, q), q)
            block = line(c, p, half_line)[j].astype(F32)
            for h in range(2):
                wide[h, at, :] = block[:, lanes(h)]

    events = [
        (d, way, half_line)
        for d in (2, 1, 3, 4)
        for half_line in range(2)
        for way in range(2)
        if d <= 3 + (way == half_line)
    ]

    def moved(c, d, way):
        return (place_of(c) + (NZ - d if way == 0 else d)) % NZ

    for c in range(2):

        @pl.when(core == c)
        def _(c=c):
            here_p = place_of(c)
            for step, half_line in ((2, 0), (2, 1), (1, 0), (1, 1)):
                part = line(c, here_p, half_line)
                for end in (step, NZ - step):
                    send(
                        part,
                        part,
                        send_sem.at[3],
                        next_sem.at[index_of(c, here_p), half_line],
                        peer(c, (here_p + end) % NZ),
                    )
            for half_line in range(2):
                part = line(c, here_p, half_line)
                send(
                    part,
                    part,
                    send_sem.at[4],
                    twin_sem.at[index_of(c, here_p), half_line],
                    twin,
                )

    await_bytes(half, left_sem.at[0])
    for h in range(2):
        half_wide[h] = half[:, :, lanes(h)].astype(F32).reshape(NZ * NS, 128)
    for b in range(NS):
        mine_send[b] = jnp.concatenate(
            [half_wide[h, pl.ds(b, NZ, stride=NS), :] for h in range(2)], axis=1
        ).astype(BF16)
    keep(mine_send.at[s], mine.at[s], left_sem.at[1])
    for t in range(1, NS):
        st = (s + t) % NS
        send(mine_send.at[st], mine.at[s], send_sem.at[2], left_sem.at[1], me.at(s=st))

    for c in range(2):

        @pl.when(core == c)
        def _(c=c):
            here_p = place_of(c)
            steps = [(here_p, 0, 0, 0), (here_p, 0, 0, 1)] + [
                (moved(c, d, way), d, way, half_line) for d, way, half_line in events
            ]
            far_p = place_of(1 - c)
            far_steps = [(far_p, 0), (far_p, 1)] + [
                (moved(1 - c, d, way), half_line) for d, way, half_line in events
            ]

            def from_twin(k):
                p, half_line = far_steps[k]
                part = line(1 - c, p, half_line)
                await_bytes(part, twin_sem.at[index_of(1 - c, p), half_line])
                widen(1 - c, p, half_line)

            for k, (p, d, way, half_line) in enumerate(steps):
                part = line(c, p, half_line)
                if d:
                    sem = next_sem.at[index_of(c, p), half_line]
                    await_bytes(part, sem)
                    if d == 2:
                        for more in range(1, 2 + (way == half_line)):
                            end = (here_p + (NZ - more if way else more)) % NZ
                            send(part, part, send_sem.at[3], sem, peer(c, end))
                    send(
                        part,
                        part,
                        send_sem.at[4],
                        twin_sem.at[index_of(c, p), half_line],
                        twin,
                    )
                widen(c, p, half_line)
                if k >= 4:
                    from_twin(k - 4)
            for k in range(len(steps) - 4, len(steps)):
                from_twin(k)

    await_bytes(mine, left_sem.at[1])

    @pl.when(here == 1)
    def _():
        await_bytes(half.at[pl.ds(0, 7)], send_sem.at[0])

    @pl.when(here == 0)
    def _():
        await_bytes(half, send_sem.at[0])

    await_bytes(every.at[pl.ds(0, 7), 0, 0], send_sem.at[1])
    await_bytes(mine.at[pl.ds(0, NS - 1)], send_sem.at[2])
    await_bytes(every.at[pl.ds(0, 7), :, 0], send_sem.at[3])
    await_bytes(every.at[:, :, 0], send_sem.at[4])


def outer_sums(mine, mine_wide, wide, stack):
    rows, factor, cols = stack.shape[0], mine.shape[2] // stack.shape[0], stack.shape[2]
    seqs = NZ * NS
    for h in range(2):
        mine_wide[h] = mine[:, :, lanes(h)].astype(F32).reshape(seqs, 128)
    left = jnp.concatenate(
        [
            jnp.concatenate(
                [mine_wide[h, pl.ds(z, NS, stride=NZ), :] for z in range(NZ)], axis=0
            ).T
            for h in range(2)
        ],
        axis=0,
    ).astype(BF16)

    @pl.loop(0, factor, unroll=4)
    def _(q):
        part = jnp.concatenate(
            [wide[h, pl.ds(q, seqs, stride=factor), :] for h in range(2)], axis=1
        ).astype(BF16)
        outer = dot(left, part) * (1.0 / seqs)
        at = pl.ds(pl.multiple_of(q * factor, factor), factor)
        stack[:, at, :] = outer.astype(BF16).reshape(rows, factor, cols)


def gated(gate, value, normed, acc, i):
    rows = acc.shape[1] // value.shape[0]
    side = jax.nn.sigmoid(dot(gate, normed)) * dot(value, normed)
    for h in range(2):
        acc[h, pl.ds(i, value.shape[0], stride=rows), :] = side[:, lanes(h)]


def put_side(acc, side):
    for h in range(2):
        side[h] = split_rows(acc[h]).reshape(side.shape[1:])


def left_gates(out_w, pair, gate_ref, value_ref, stack, mid_all, normed_all, acc, side):
    gate, value = turned(gate_ref), turned(value_ref)

    @pl.loop(0, pair.shape[0], unroll=2)
    def _(i):
        mid = (dot(out_w[...], stack[i]) + pair[i].astype(F32).T).astype(BF16)
        mid_all[i] = mid
        normed = layer_norm(mid, 0).astype(BF16)
        normed_all[i] = normed
        gated(gate, value, normed, acc, i)

    put_side(acc, side)


def right_gates(gate_ref, value_ref, normed_all, acc, side):
    gate, value = turned(gate_ref), turned(value_ref)

    @pl.loop(0, normed_all.shape[0], unroll=2)
    def _(i):
        gated(gate, value, normed_all[i], acc, i)

    put_side(acc, side)


def along_y(me, src, dst, send_sem, sem, offsets=range(NS)):
    for t in offsets:
        if t == 0:
            keep(src(me.s), dst, sem)
        else:
            st = (me.s + t) % NS
            send(src(st), dst, send_sem, sem, me.at(s=st))


def along_z(me, src, dst, send_sem, sem, offsets=(0,) + HOPS):
    for t in offsets:
        if t == 0:
            keep(src(me.z), dst, sem)
        else:
            zt = (me.z + t) % NZ
            send(src(zt), dst, send_sem, sem, me.at(z=zt))


ORDER = (0,) + HOPS
UNITS = NZ + NS
LAG = 8


def left_legs(me, side, y_mid, z_mid, out, sems):
    send_sem, first_sem, z_sem, s_sem = sems
    await_bytes(y_mid, first_sem.at[0])
    along_z(me, lambda zt: y_mid.at[:, zt], out.at[0, me.z], send_sem.at[2], z_sem.at[me.z])
    await_bytes(z_mid, first_sem.at[1])
    along_y(me, lambda st: z_mid.at[:, st], out.at[1, :, me.s], send_sem.at[3], s_sem.at[me.s])


def first_legs(me, side, y_mid, z_mid, send_sem, first_sem, parts=(0, 1)):
    for part in parts:
        along_y(
            me,
            lambda st: side.at[0, :, st],
            y_mid.at[me.s],
            send_sem.at[0],
            first_sem.at[0],
            range(part, NS, 2),
        )
        along_z(
            me,
            lambda zt: side.at[1, zt],
            z_mid.at[me.z],
            send_sem.at[1],
            first_sem.at[1],
            ORDER[4 * part : 4 * part + 4],
        )


def legs_left(y_mid, z_mid, send_sem):
    await_bytes(y_mid.at[pl.ds(0, NS - 1)], send_sem.at[0])
    await_bytes(z_mid.at[pl.ds(0, NZ - 1)], send_sem.at[1])
    await_bytes(y_mid.at[:, pl.ds(0, NZ - 1)], send_sem.at[2])
    await_bytes(z_mid.at[:, pl.ds(0, NS - 1)], send_sem.at[3])


def spread(
    me, left_side, right_side, right_gates, output_gates, a_out, rows_all, b_all, b_out, mids, l_sems, r_sems, x_sems
):
    z, s, x = me.z, me.s, me.x
    ly_mid, lz_mid, ry_mid, rz_mid = mids
    x_send, near_sem, far_sem, side_sem = x_sems
    first_legs(me, left_side, ly_mid, lz_mid, l_sems[0], l_sems[1])
    right_gates()
    first_legs(me, right_side, ry_mid, rz_mid, r_sems[0], r_sems[1], (0,))
    output_gates()
    left_legs(me, left_side, ly_mid, lz_mid, a_out.at[:, x], l_sems)
    first_legs(me, right_side, ry_mid, rz_mid, r_sems[0], r_sems[1], (1,))

    after, before = (x + 1) % NX, (x + 3) % NX

    def unit(k):
        if k < NZ:
            zt = (z + ORDER[k]) % NZ
            return zt, lambda xt: a_out.at[0, xt, zt], l_sems[2].at[zt]
        st = (s + 2 * NS - k + NZ) % NS
        return NZ + st, lambda xt: a_out.at[1, xt, :, st], l_sems[3].at[st]

    def pass_on(k):
        n, place, _ = unit(k)
        way = k % 2
        part = place(after if way else before)
        await_bytes(part, near_sem.at[way, n])
        send(part, part, x_send.at[1], far_sem.at[n], me.at(x=before if way else after))

    for k in range(UNITS):
        n, place, sem = unit(k)
        part = place(x)
        await_bytes(part, sem)
        send(part, part, x_send.at[0], near_sem.at[0, n], me.at(x=after))
        send(part, part, x_send.at[0], near_sem.at[1, n], me.at(x=before))
        if k >= LAG:
            pass_on(k - LAG)
        if k == UNITS - 8:
            left_legs(me, right_side, ry_mid, rz_mid, b_all, r_sems)
    for k in range(UNITS - LAG, UNITS):
        pass_on(k)

    for k in range(NZ):
        zt = (z + ORDER[k]) % NZ
        xt = zt // 2
        part, there = b_all.at[0, zt], b_out.at[0, x, zt % 2]
        await_bytes(part, r_sems[2].at[zt])

        @pl.when(xt == x)
        def _():
            keep(part, there, side_sem)

        @pl.when(xt != x)
        def _():
            send(part, there, x_send.at[2], side_sem, me.at(x=xt))

        for u in (2 * k, 2 * k + 1):
            su = (s + NS - u) % NS
            await_bytes(b_all.at[1, :, su], r_sems[3].at[su])
            for d in (1, 3, 2):
                xt = (x + d) % NX
                send(
                    b_all.at[1, pl.ds(2 * xt, 2), su],
                    b_out.at[1, x, :, su],
                    x_send.at[2],
                    side_sem,
                    me.at(x=xt),
                )
    keep(b_all.at[1, pl.ds(2 * x, 2)], b_out.at[1, x], side_sem)

    for k in range(UNITS):
        n, place, _ = unit(k)
        part = place(x)
        await_bytes(part, far_sem.at[n])
        await_bytes(part, near_sem.at[1 - k % 2, n])

    @pl.loop(0, NZ)
    def _(zt):
        for k in range(NX):
            for h in range(2):
                rows_all[zt, :, lanes(2 * k + h)] = flat_rows(a_out.at[h, k, zt])

    await_bytes(b_out, side_sem)


def multiply_and_return(me, rows_all, b_out, cols_all, product, y_mid, z_mid, final, sems):
    send_sem, first_sem, final_sem = sems
    z, s = me.z, me.s
    for k in range(NX):
        for h in range(2):
            cols_all[:, lanes(2 * k + h)] = flat_rows(b_out.at[h, k])
    for couple in ((0, 1), (7, 2), (6, 3), (5, 4)):
        rows = jnp.concatenate([rows_all[(z + t) % NZ] for t in couple], axis=0)
        total = lax.dot_general(
            rows, cols_all[...], (((1,), (1,)), ((), ())), preferred_element_type=F32
        )
        count = total.shape[0] // 2
        for n, t in enumerate(couple):
            zt = (z + t) % NZ
            block = total[n * count : (n + 1) * count]
            for h in range(2):
                product[h, zt] = split_rows(block[:, lanes(h)])
            if t == 0:
                keep(product.at[1, z], z_mid.at[z], first_sem.at[1])
            else:
                send(product.at[1, zt], z_mid.at[z], send_sem.at[1], first_sem.at[1], me.at(z=zt))
    along_y(me, lambda st: product.at[0, :, st], y_mid.at[s], send_sem.at[0], first_sem.at[0])
    await_bytes(z_mid, first_sem.at[1])
    along_y(me, lambda st: z_mid.at[:, st], final.at[1, :, s], send_sem.at[3], final_sem)
    await_bytes(y_mid, first_sem.at[0])
    along_z(me, lambda zt: y_mid.at[:, zt], final.at[0, z], send_sem.at[2], final_sem)
    await_bytes(final, final_sem)


def output_gates(gate_ref, normed_all, gate_all):
    gate = turned(gate_ref)

    @pl.loop(0, normed_all.shape[0], unroll=2)
    def _(i):
        gate_all[i] = jax.nn.sigmoid(dot(gate, normed_all[i]))


def finish(parts, wide, mid_all, gate_all, out_ref, rows_out, result, sem):
    rows, width, cols = mid_all.shape
    for h in range(2):
        wide[h] = parts[h].astype(F32).reshape(-1, 128)
    hidden = wide.shape[1] // rows
    out_w = turned(out_ref)

    @pl.loop(0, rows, unroll=4)
    def _(i):
        product = jnp.concatenate(
            [wide[h, pl.ds(i, hidden, stride=rows), :] for h in range(2)], axis=1
        )
        normed = layer_norm(product, 0).astype(BF16)
        update = gate_all[i] * dot(out_w, normed)
        rows_out[i] = (mid_all[i].astype(F32) + update).T.astype(BF16)
        keep(rows_out.at[i], result.at[i], sem)

    await_bytes(rows_out, sem)


def kernel(
    pair_hbm,
    opm_out_hbm,
    align_ref,
    opm_left_ref,
    opm_right_ref,
    tri_left_ref,
    tri_left_gate_ref,
    tri_right_ref,
    tri_right_gate_ref,
    tri_gate_ref,
    tri_out_ref,
    result,
    pair,
    opm_out,
    opm_wide,
    out_w,
    normed_seq,
    left_own,
    right_own,
    half,
    half_wide,
    mine_send,
    mine,
    every,
    wide,
    stack,
    mid_all,
    normed_all,
    acc,
    left_side,
    right_side,
    ly_mid,
    lz_mid,
    ry_mid,
    rz_mid,
    py_mid,
    pz_mid,
    b_all,
    a_out,
    rows_all,
    b_out,
    cols_all,
    product,
    final,
    gate_all,
    rows_out,
    load_sem,
    g_send,
    g_first,
    g_next,
    g_twin,
    g_left,
    l_send,
    l_first,
    l_z,
    l_s,
    r_send,
    r_first,
    r_z,
    r_s,
    x_send,
    x_near,
    x_far,
    x_side,
    p_send,
    p_first,
    p_final,
    out_sem,
):
    me = Place()
    count = greet_all(me)
    keep(pair_hbm, pair, load_sem.at[0])
    keep(opm_out_hbm, opm_out, load_sem.at[1])
    factors(align_ref, opm_left_ref, opm_right_ref, normed_seq, left_own, right_own)
    await_bytes(opm_out, load_sem.at[1])
    await_bytes(pair, load_sem.at[0])
    opm_wide[...] = opm_out[...].astype(F32)
    p = opm_left_ref.shape[0]
    q = opm_right_ref.shape[0]
    for k in range(q):
        rows = opm_wide[pl.ds(k, p, stride=q), :]
        mine_rows = slice(k * p, (k + 1) * p)
        stack[0, mine_rows, 0:128] = rows.astype(BF16)
    out_w[...] = stack[0, :, 0:128].astype(F32).T.astype(BF16)
    pl.semaphore_wait(pltpu.get_barrier_semaphore(), count)

    gather(
        me,
        left_own,
        right_own,
        half,
        half_wide,
        mine_send,
        mine,
        every,
        wide,
        (g_send, g_first, g_next, g_twin, g_left),
    )
    outer_sums(mine, half_wide, wide, stack)
    left_gates(
        out_w,
        pair,
        tri_left_gate_ref,
        tri_left_ref,
        stack,
        mid_all,
        normed_all,
        acc.at[0],
        left_side,
    )
    spread(
        me,
        left_side,
        right_side,
        lambda: right_gates(
            tri_right_gate_ref, tri_right_ref, normed_all, acc.at[1], right_side
        ),
        lambda: output_gates(tri_gate_ref, normed_all, gate_all),
        a_out,
        rows_all,
        b_all,
        b_out,
        (ly_mid, lz_mid, ry_mid, rz_mid),
        (l_send, l_first, l_z, l_s),
        (r_send, r_first, r_z, r_s),
        (x_send, x_near, x_far, x_side),
    )
    multiply_and_return(
        me, rows_all, b_out, cols_all, product, py_mid, pz_mid, final, (p_send, p_first, p_final)
    )
    finish(final, acc.at[0], mid_all, gate_all, tri_out_ref, rows_out, result, out_sem)
    legs_left(ly_mid, lz_mid, l_send)
    legs_left(ry_mid, rz_mid, r_send)
    await_bytes(a_out.at[:, pl.ds(0, 2)], x_send.at[0])
    await_bytes(a_out.at[:, 0], x_send.at[1])
    await_bytes(b_out.at[:, pl.ds(0, NX - 1)], x_send.at[2])
    legs_left(py_mid, pz_mid, p_send)


def on_device(pair, alignment, opm_left, opm_right, opm_out, *weights):
    rows, cols, width = pair.shape
    model = alignment.shape[2]
    factor = opm_left.shape[1]
    hidden = weights[0].shape[1]
    seqs = NZ * NS

    def vb(*shape):
        return pltpu.VMEM(shape, BF16)

    def vf(*shape):
        return pltpu.VMEM(shape, F32)

    scratch = [
        vb(rows, cols, width),
        vb(factor * factor, width),
        vf(factor * factor, width),
        vb(width, factor * factor),
        vf(model // 128, cols, 128),
        vb(2, NS, rows * factor),
        vb(factor, cols),
        vb(NZ, NS, rows * factor),
        vf(2, seqs, 128),
        vb(NS, NZ, rows * factor),
        vb(NS, NZ, rows * factor),
        vb(NZ, NY, 2, factor, cols),
        vf(2, seqs * factor, 128),
        vb(rows, factor * factor, cols),
        vb(rows, width, cols),
        vb(rows, width, cols),
        vf(2, 2, hidden * rows, 128),
        vb(2, NZ, NS, rows, 128),
        vb(2, NZ, NS, rows, 128),
        vb(NS, NZ, rows, 128),
        vb(NZ, NS, rows, 128),
        vb(NS, NZ, rows, 128),
        vb(NZ, NS, rows, 128),
        vb(NS, NZ, rows, 128),
        vb(NZ, NS, rows, 128),
        vb(2, NZ, NS, rows, 128),
        vb(2, NX, NZ, NS, rows, 128),
        vb(NZ, NS * rows, NX * cols),
        vb(2, NX, NZ // NX, NS, rows, 128),
        vb(cols, NX * cols),
        vb(2, NZ, NS, rows, 128),
        vb(2, NZ, NS, rows, 128),
        vf(rows, width, cols),
        vb(rows, cols, width),
        DMA((2,)),
        DMA((5,)),
        DMA,
        DMA((8, 2)),
        DMA((8, 2)),
        DMA((2,)),
        DMA((4,)),
        DMA((2,)),
        DMA((NZ,)),
        DMA((NS,)),
        DMA((4,)),
        DMA((2,)),
        DMA((NZ,)),
        DMA((NS,)),
        DMA((3,)),
        DMA((2, UNITS)),
        DMA((UNITS,)),
        DMA,
        DMA((4,)),
        DMA((2,)),
        DMA,
        DMA,
    ]
    return pl.pallas_call(
        kernel,
        out_shape=jax.ShapeDtypeStruct((rows, cols, width), BF16),
        in_specs=[ANY, ANY] + [VMEM] * 9,
        out_specs=ANY,
        scratch_shapes=scratch,
        compiler_params=pltpu.CompilerParams(
            collective_id=0, has_side_effects=True, vmem_limit_bytes=56 << 20
        ),
        name="evoformer_pair",
    )(pair, opm_out, alignment, opm_left.T, opm_right.T, *weights)


def solution(mesh):
    split = P(("row", "seq"), "col", None)
    return jax.shard_map(
        on_device,
        mesh=mesh,
        in_specs=(split, split) + (P(),) * 9,
        out_specs=split,
        check_vma=False,
    )
```

```python
import jax
import jax.numpy as jnp
from jax import lax
from jax.experimental import pallas as pl
from jax.experimental.pallas import tpu as pltpu
from jax.sharding import PartitionSpec as P

EPS = 1e-05
MESH = pl.DeviceIdType.MESH
F32 = jnp.float32
BF16 = jnp.bfloat16
VMEM = pl.BlockSpec(memory_space=pltpu.VMEM)
ANY = pl.BlockSpec(memory_space=pl.ANY)
DMA = pltpu.SemaphoreType.DMA

NX = 4
NZ = 8
NQ = 8
NS = 2 * NQ
NY = NS // 2
HOPS = (1, 7, 2, 6, 3, 5, 4)


class Place:
    def __init__(self):
        row = lax.axis_index("row")
        self.x = lax.axis_index("col")
        seq = lax.axis_index("seq")
        self.z = row // 2
        self.s = (row % 2) * NQ + seq
        self.yy = self.s // 2
        self.core = self.s % 2

    def at(self, z=None, s=None, x=None):
        z = self.z if z is None else z
        s = self.s if s is None else s
        x = self.x if x is None else x
        return (z * 2 + s // NQ, x, s % NQ)


def send(src, dst, send_sem, recv_sem, device):
    pltpu.make_async_remote_copy(
        src_ref=src,
        dst_ref=dst,
        send_sem=send_sem,
        recv_sem=recv_sem,
        device_id=device,
        device_id_type=MESH,
    ).start()


def keep(src, dst, sem):
    pltpu.make_async_copy(src, dst, sem).start()


def await_bytes(ref, sem):
    pltpu.make_async_copy(ref, ref, sem).wait()


def greet(device):
    pl.semaphore_signal(
        pltpu.get_barrier_semaphore(), inc=1, device_id=device, device_id_type=MESH
    )


def layer_norm(values, axis):
    values = values.astype(F32)
    center = values - jnp.mean(values, axis=axis, keepdims=True)
    spread = jnp.mean(center * center, axis=axis, keepdims=True)
    return center * lax.rsqrt(spread + EPS)


def turned(ref):
    return ref[...].astype(F32).T.astype(BF16)


def dot(a, b):
    return jnp.dot(a, b, preferred_element_type=F32)


def lanes(h):
    return slice(h * 128, (h + 1) * 128)


def flat_rows(ref):
    values = ref[...].astype(F32)
    return values.reshape(-1, values.shape[-1]).astype(BF16)


def split_rows(values):
    return values.reshape(-1, 8, values.shape[-1]).astype(BF16)


def factors(align_ref, wl_ref, wr_ref, normed, left_own, right_own):
    cols, width = align_ref.shape[1:]
    p = wl_ref.shape[0]
    seq = layer_norm(align_ref[0], 1).astype(BF16)
    right_own[...] = lax.dot_general(
        wr_ref[...], seq, (((1,), (1,)), ((), ())), preferred_element_type=F32
    ).astype(BF16)
    wide = seq.astype(F32)
    for h in range(width // 128):
        normed[h] = wide[:, lanes(h)]
    lane = lax.broadcasted_iota(jnp.int32, (p, 8 * p), 1)
    unit = lax.broadcasted_iota(jnp.int32, (p, 8 * p), 0)
    tile = jnp.where(lane % p == unit, 1.0, 0.0).astype(BF16)
    repeated = dot(turned(wl_ref), tile)
    group = lax.broadcasted_iota(jnp.int32, repeated.shape, 1) // p
    total = None
    for i in range(8):
        rows = jnp.concatenate(
            [normed[h, pl.ds(i, cols // 8, stride=8), :] for h in range(width // 128)], axis=1
        ).astype(BF16)
        term = dot(rows, jnp.where(group == i, repeated, 0.0).astype(BF16))
        total = term if total is None else total + term
    left_own[...] = total.astype(BF16).reshape(left_own.shape)


def greet_all(me):
    for t in range(1, NS):
        greet(me.at(s=(me.s + t) % NS))
    for t in range(1, NZ):
        greet(me.at(z=(me.z + t) % NZ))
    for t in range(1, NX):
        greet(me.at(x=(me.x + t) % NX))
    owner = me.z // 2
    for t in range(NZ):

        @pl.when(jnp.logical_not(jnp.logical_and(owner == me.x, me.z == t)))
        def _():
            greet(me.at(z=t, x=owner))

    return NS - 1 + NZ - 1 + NX - 1 + 8 - jnp.where(owner == me.x, 1, 0)


def gather(me, left_own, right_own, half, half_wide, mine_send, mine, every, wide, sems):
    send_sem, first_sem, next_sem, twin_sem, left_sem = sems
    z, s, x, yy, core = me.z, me.s, me.x, me.yy, me.core
    q = right_own.shape[0]
    here = jnp.where(z // 2 == x, 1, 0)

    own = every.at[z, yy, core]
    keep(right_own, own, first_sem)

    @pl.when(core == 0)
    def _():
        for t in HOPS:
            send(right_own, own, send_sem.at[1], first_sem, me.at(z=(z + t) % NZ))

    @pl.when(core == 1)
    def _():
        for t in HOPS:
            send(right_own, own, send_sem.at[1], first_sem, me.at(s=(s + 2 * t) % NS))

    for h in range(2):
        for xt in range(NX):
            zt = 2 * x + h
            same = jnp.logical_and(x == xt, z == zt)

            @pl.when(same)
            def _():
                keep(left_own.at[h], half.at[z], left_sem.at[0])

            @pl.when(jnp.logical_not(same))
            def _():
                send(left_own.at[h], half.at[z], send_sem.at[0], left_sem.at[0], me.at(z=zt, x=xt))

    await_bytes(every.at[:, 0, 0], first_sem)
    twin = me.at(s=s + 1 - 2 * core)

    def line(c, p, half_line):
        at = pl.ds(4 * half_line, 4)
        return every.at[at, index_of(c, p), 0] if c == 0 else every.at[index_of(c, p), at, 1]

    def index_of(c, p):
        return p % 2 * 4 + p // 2 if c == 0 else p

    def place_of(c):
        return yy % 4 * 2 + yy // 4 if c == 0 else z

    def peer(c, p):
        return me.at(s=2 * index_of(c, p)) if c == 0 else me.at(z=p)

    def widen(c, p, half_line):
        @pl.loop(0, 4)
        def _(j):
            n = (4 * half_line + j) * NS + 2 * index_of(c, p)
            if c == 1:
                n = index_of(c, p) * NS + 2 * (4 * half_line + j) + 1
            at = pl.ds(pl.multiple_of(n * q, q), q)
            block = line(c, p, half_line)[j].astype(F32)
            for h in range(2):
                wide[h, at, :] = block[:, lanes(h)]

    events = [
        (d, way, half_line)
        for d in (2, 1, 3, 4)
        for half_line in range(2)
        for way in range(2)
        if d <= 3 + (way == half_line)
    ]

    def moved(c, d, way):
        return (place_of(c) + (NZ - d if way == 0 else d)) % NZ

    for c in range(2):

        @pl.when(core == c)
        def _(c=c):
            here_p = place_of(c)
            for step, half_line in ((2, 0), (2, 1), (1, 0), (1, 1)):
                part = line(c, here_p, half_line)
                for end in (step, NZ - step):
                    send(
                        part,
                        part,
                        send_sem.at[3],
                        next_sem.at[index_of(c, here_p), half_line],
                        peer(c, (here_p + end) % NZ),
                    )
            for half_line in range(2):
                part = line(c, here_p, half_line)
                send(
                    part,
                    part,
                    send_sem.at[4],
                    twin_sem.at[index_of(c, here_p), half_line],
                    twin,
                )

    await_bytes(half, left_sem.at[0])
    for h in range(2):
        half_wide[h] = half[:, :, lanes(h)].astype(F32).reshape(NZ * NS, 128)
    for b in range(NS):
        mine_send[b] = jnp.concatenate(
            [half_wide[h, pl.ds(b, NZ, stride=NS), :] for h in range(2)], axis=1
        ).astype(BF16)
    keep(mine_send.at[s], mine.at[s], left_sem.at[1])
    for t in range(1, NS):
        st = (s + t) % NS
        send(mine_send.at[st], mine.at[s], send_sem.at[2], left_sem.at[1], me.at(s=st))

    for c in range(2):

        @pl.when(core == c)
        def _(c=c):
            here_p = place_of(c)
            steps = [(here_p, 0, 0, 0), (here_p, 0, 0, 1)] + [
                (moved(c, d, way), d, way, half_line) for d, way, half_line in events
            ]
            far_p = place_of(1 - c)
            far_steps = [(far_p, 0), (far_p, 1)] + [
                (moved(1 - c, d, way), half_line) for d, way, half_line in events
            ]

            def from_twin(k):
                p, half_line = far_steps[k]
                part = line(1 - c, p, half_line)
                await_bytes(part, twin_sem.at[index_of(1 - c, p), half_line])
                widen(1 - c, p, half_line)

            for k, (p, d, way, half_line) in enumerate(steps):
                part = line(c, p, half_line)
                if d:
                    sem = next_sem.at[index_of(c, p), half_line]
                    await_bytes(part, sem)
                    if d == 2:
                        for more in range(1, 2 + (way == half_line)):
                            end = (here_p + (NZ - more if way else more)) % NZ
                            send(part, part, send_sem.at[3], sem, peer(c, end))
                    send(
                        part,
                        part,
                        send_sem.at[4],
                        twin_sem.at[index_of(c, p), half_line],
                        twin,
                    )
                widen(c, p, half_line)
                if k >= 4:
                    from_twin(k - 4)
            for k in range(len(steps) - 4, len(steps)):
                from_twin(k)

    await_bytes(mine, left_sem.at[1])

    @pl.when(here == 1)
    def _():
        await_bytes(half.at[pl.ds(0, 7)], send_sem.at[0])

    @pl.when(here == 0)
    def _():
        await_bytes(half, send_sem.at[0])

    await_bytes(every.at[pl.ds(0, 7), 0, 0], send_sem.at[1])
    await_bytes(mine.at[pl.ds(0, NS - 1)], send_sem.at[2])
    await_bytes(every.at[pl.ds(0, 7), :, 0], send_sem.at[3])
    await_bytes(every.at[:, :, 0], send_sem.at[4])


def outer_sums(mine, mine_wide, wide, stack):
    rows, factor, cols = stack.shape[0], mine.shape[2] // stack.shape[0], stack.shape[2]
    seqs = NZ * NS
    for h in range(2):
        mine_wide[h] = mine[:, :, lanes(h)].astype(F32).reshape(seqs, 128)
    left = jnp.concatenate(
        [
            jnp.concatenate(
                [mine_wide[h, pl.ds(z, NS, stride=NZ), :] for z in range(NZ)], axis=0
            ).T
            for h in range(2)
        ],
        axis=0,
    )
    left = (left * (1.0 / seqs)).astype(BF16)

    @pl.loop(0, factor, unroll=4)
    def _(q):
        part = jnp.concatenate(
            [wide[h, pl.ds(q, seqs, stride=factor), :] for h in range(2)], axis=1
        ).astype(BF16)
        outer = dot(left, part)
        at = pl.ds(pl.multiple_of(q * factor, factor), factor)
        stack[:, at, :] = outer.astype(BF16).reshape(rows, factor, cols)


def gated(gate, value, normed, acc, i):
    rows = acc.shape[1] // value.shape[0]
    side = jax.nn.sigmoid(dot(gate, normed)) * dot(value, normed)
    for h in range(2):
        acc[h, pl.ds(i, value.shape[0], stride=rows), :] = side[:, lanes(h)]


def put_side(acc, side):
    for h in range(2):
        side[h] = split_rows(acc[h]).reshape(side.shape[1:])


def left_gates(out_w, pair, gate, value, stack, mid_all, normed_all, acc, side):
    gate, value = gate[...], value[...]

    @pl.loop(0, pair.shape[0], unroll=2)
    def _(i):
        mid = (dot(out_w[...], stack[i]) + pair[i]).astype(BF16)
        mid_all[i] = mid
        normed = layer_norm(mid, 0).astype(BF16)
        normed_all[i] = normed
        gated(gate, value, normed, acc, i)

    put_side(acc, side)


def right_gates(gate, value, normed_all, acc, side):
    gate, value = gate[...], value[...]

    @pl.loop(0, normed_all.shape[0], unroll=2)
    def _(i):
        gated(gate, value, normed_all[i], acc, i)

    put_side(acc, side)


def along_y(me, src, dst, send_sem, sem, offsets=range(NS)):
    for t in offsets:
        if t == 0:
            keep(src(me.s), dst, sem)
        else:
            st = (me.s + t) % NS
            send(src(st), dst, send_sem, sem, me.at(s=st))


def along_z(me, src, dst, send_sem, sem, offsets=(0,) + HOPS):
    for t in offsets:
        if t == 0:
            keep(src(me.z), dst, sem)
        else:
            zt = (me.z + t) % NZ
            send(src(zt), dst, send_sem, sem, me.at(z=zt))


ORDER = (0,) + HOPS
UNITS = NZ + NS
LAG = 8


def left_legs(me, side, y_mid, z_mid, out, sems):
    send_sem, first_sem, z_sem, s_sem = sems
    await_bytes(y_mid, first_sem.at[0])
    along_z(me, lambda zt: y_mid.at[:, zt], out.at[0, me.z], send_sem.at[2], z_sem.at[me.z])
    await_bytes(z_mid, first_sem.at[1])
    along_y(me, lambda st: z_mid.at[:, st], out.at[1, :, me.s], send_sem.at[3], s_sem.at[me.s])


def first_legs(me, side, y_mid, z_mid, send_sem, first_sem, parts=(0, 1)):
    for part in parts:
        along_y(
            me,
            lambda st: side.at[0, :, st],
            y_mid.at[me.s],
            send_sem.at[0],
            first_sem.at[0],
            range(part, NS, 2),
        )
        along_z(
            me,
            lambda zt: side.at[1, zt],
            z_mid.at[me.z],
            send_sem.at[1],
            first_sem.at[1],
            ORDER[4 * part : 4 * part + 4],
        )


def legs_left(y_mid, z_mid, send_sem):
    await_bytes(y_mid.at[pl.ds(0, NS - 1)], send_sem.at[0])
    await_bytes(z_mid.at[pl.ds(0, NZ - 1)], send_sem.at[1])
    await_bytes(y_mid.at[:, pl.ds(0, NZ - 1)], send_sem.at[2])
    await_bytes(z_mid.at[:, pl.ds(0, NS - 1)], send_sem.at[3])


def spread(
    me, left_side, right_side, right_gates, output_gates, a_out, rows_all, b_all, b_out, mids, l_sems, r_sems, x_sems
):
    z, s, x = me.z, me.s, me.x
    ly_mid, lz_mid, ry_mid, rz_mid = mids
    x_send, near_sem, far_sem, side_sem = x_sems
    first_legs(me, left_side, ly_mid, lz_mid, l_sems[0], l_sems[1])
    right_gates()
    first_legs(me, right_side, ry_mid, rz_mid, r_sems[0], r_sems[1], (0,))
    output_gates()
    left_legs(me, left_side, ly_mid, lz_mid, a_out.at[:, x], l_sems)
    first_legs(me, right_side, ry_mid, rz_mid, r_sems[0], r_sems[1], (1,))

    after, before = (x + 1) % NX, (x + 3) % NX

    def unit(k):
        if k < NZ:
            zt = (z + ORDER[k]) % NZ
            return zt, lambda xt: a_out.at[0, xt, zt], l_sems[2].at[zt]
        st = (s + 2 * NS - k + NZ) % NS
        return NZ + st, lambda xt: a_out.at[1, xt, :, st], l_sems[3].at[st]

    def pass_on(k):
        n, place, _ = unit(k)
        way = k % 2
        part = place(after if way else before)
        await_bytes(part, near_sem.at[way, n])
        send(part, part, x_send.at[1], far_sem.at[n], me.at(x=before if way else after))

    for k in range(UNITS):
        n, place, sem = unit(k)
        part = place(x)
        await_bytes(part, sem)
        send(part, part, x_send.at[0], near_sem.at[0, n], me.at(x=after))
        send(part, part, x_send.at[0], near_sem.at[1, n], me.at(x=before))
        if k >= LAG:
            pass_on(k - LAG)
        if k == UNITS - 8:
            left_legs(me, right_side, ry_mid, rz_mid, b_all, r_sems)
    for k in range(UNITS - LAG, UNITS):
        pass_on(k)

    for k in range(NZ):
        zt = (z + ORDER[k]) % NZ
        xt = zt // 2
        part, there = b_all.at[0, zt], b_out.at[0, x, zt % 2]
        await_bytes(part, r_sems[2].at[zt])

        @pl.when(xt == x)
        def _():
            keep(part, there, side_sem)

        @pl.when(xt != x)
        def _():
            send(part, there, x_send.at[2], side_sem, me.at(x=xt))

        for u in (2 * k, 2 * k + 1):
            su = (s + NS - u) % NS
            await_bytes(b_all.at[1, :, su], r_sems[3].at[su])
            for d in (1, 3, 2):
                xt = (x + d) % NX
                send(
                    b_all.at[1, pl.ds(2 * xt, 2), su],
                    b_out.at[1, x, :, su],
                    x_send.at[2],
                    side_sem,
                    me.at(x=xt),
                )
    keep(b_all.at[1, pl.ds(2 * x, 2)], b_out.at[1, x], side_sem)

    for k in range(UNITS):
        n, place, _ = unit(k)
        part = place(x)
        await_bytes(part, far_sem.at[n])
        await_bytes(part, near_sem.at[1 - k % 2, n])

    @pl.loop(0, NZ)
    def _(zt):
        for k in range(NX):
            for h in range(2):
                rows_all[zt, :, lanes(2 * k + h)] = flat_rows(a_out.at[h, k, zt])

    await_bytes(b_out, side_sem)


def multiply_and_return(me, rows_all, b_out, cols_all, product, y_mid, z_mid, final, sems):
    send_sem, first_sem, final_sem = sems
    z, s = me.z, me.s
    for k in range(NX):
        for h in range(2):
            cols_all[:, lanes(2 * k + h)] = flat_rows(b_out.at[h, k])
    for couple in ((0, 1), (7, 2), (6, 3), (5, 4)):
        rows = jnp.concatenate([rows_all[(z + t) % NZ] for t in couple], axis=0)
        total = lax.dot_general(
            rows, cols_all[...], (((1,), (1,)), ((), ())), preferred_element_type=F32
        )
        count = total.shape[0] // 2
        for n, t in enumerate(couple):
            zt = (z + t) % NZ
            block = total[n * count : (n + 1) * count]
            for h in range(2):
                product[h, zt] = split_rows(block[:, lanes(h)])
    same = s // NQ * NQ
    starts = (same, NQ - same)

    def first(chunk):
        near = pl.ds(pl.multiple_of(starts[chunk], NQ), NQ)
        along_z(
            me,
            lambda zt: product.at[1, zt, near],
            z_mid.at[z, near],
            send_sem.at[1],
            first_sem.at[1, chunk],
        )
        for t in range(chunk, NZ, 2):
            zt = (z + t) % NZ
            along_y(
                me,
                lambda st: product.at[0, zt, st],
                y_mid.at[s, zt],
                send_sem.at[0],
                first_sem.at[0, chunk],
            )

    def second(chunk):
        await_bytes(z_mid.at[:, pl.ds(0, NQ)], first_sem.at[1, chunk])
        base = starts[chunk]
        for t in range(NQ):
            st = base + (s + t) % NQ
            part, there = z_mid.at[:, st], final.at[1, :, s]
            if t == 0 and chunk == 0:
                keep(part, there, final_sem)
            else:
                send(part, there, send_sem.at[3], final_sem, me.at(s=st))
        await_bytes(y_mid.at[:, pl.ds(0, NZ // 2)], first_sem.at[0, chunk])
        along_z(
            me,
            lambda zt: y_mid.at[:, zt],
            final.at[0, z],
            send_sem.at[2],
            final_sem,
            (0, 2, 6, 4) if chunk == 0 else (1, 7, 3, 5),
        )

    first(0)
    first(1)
    second(0)
    second(1)
    await_bytes(final, final_sem)


def output_gates(gate, normed_all, gate_all):
    gate = gate[...]

    @pl.loop(0, normed_all.shape[0], unroll=2)
    def _(i):
        gate_all[i] = jax.nn.sigmoid(dot(gate, normed_all[i]))


def finish(parts, wide, mid_all, gate_all, out_w, rows_out, result, sem):
    rows, width, cols = mid_all.shape
    for h in range(2):
        wide[h] = parts[h].astype(F32).reshape(-1, 128)
    hidden = wide.shape[1] // rows
    out_w = out_w[...]

    @pl.loop(0, rows, unroll=4)
    def _(i):
        product = jnp.concatenate(
            [wide[h, pl.ds(i, hidden, stride=rows), :] for h in range(2)], axis=1
        )
        normed = layer_norm(product, 0).astype(BF16)
        update = gate_all[i] * dot(out_w, normed)
        rows_out[i] = (mid_all[i].astype(F32) + update).T.astype(BF16)
        keep(rows_out.at[i], result.at[i], sem)

    await_bytes(rows_out, sem)


def kernel(
    pair_hbm,
    opm_out_hbm,
    align_ref,
    opm_left_ref,
    opm_right_ref,
    tri_left_ref,
    tri_left_gate_ref,
    tri_right_ref,
    tri_right_gate_ref,
    tri_gate_ref,
    tri_out_ref,
    result,
    pair,
    opm_out,
    opm_wide,
    out_w,
    normed_seq,
    left_own,
    right_own,
    half,
    half_wide,
    mine_send,
    mine,
    every,
    wide,
    stack,
    mid_all,
    normed_all,
    acc,
    left_side,
    right_side,
    ly_mid,
    lz_mid,
    ry_mid,
    rz_mid,
    py_mid,
    pz_mid,
    b_all,
    a_out,
    rows_all,
    b_out,
    cols_all,
    product,
    final,
    gate_all,
    rows_out,
    pair_wide,
    turned_all,
    load_sem,
    g_send,
    g_first,
    g_next,
    g_twin,
    g_left,
    l_send,
    l_first,
    l_z,
    l_s,
    r_send,
    r_first,
    r_z,
    r_s,
    x_send,
    x_near,
    x_far,
    x_side,
    p_send,
    p_first,
    p_final,
    out_sem,
):
    me = Place()
    count = greet_all(me)
    keep(pair_hbm, pair, load_sem.at[0])
    keep(opm_out_hbm, opm_out, load_sem.at[1])
    factors(align_ref, opm_left_ref, opm_right_ref, normed_seq, left_own, right_own)
    await_bytes(opm_out, load_sem.at[1])
    await_bytes(pair, load_sem.at[0])
    opm_wide[...] = opm_out[...].astype(F32)
    p = opm_left_ref.shape[0]
    q = opm_right_ref.shape[0]
    for k in range(q):
        rows = opm_wide[pl.ds(k, p, stride=q), :]
        mine_rows = slice(k * p, (k + 1) * p)
        stack[0, mine_rows, 0:128] = rows.astype(BF16)
    out_w[...] = stack[0, :, 0:128].astype(F32).T.astype(BF16)
    for k, ref in enumerate(
        (
            tri_left_ref,
            tri_left_gate_ref,
            tri_right_ref,
            tri_right_gate_ref,
            tri_gate_ref,
            tri_out_ref,
        )
    ):
        turned_all[k] = turned(ref)

    @pl.loop(0, pair.shape[0])
    def _(i):
        pair_wide[i] = pair[i].astype(F32).T

    pl.semaphore_wait(pltpu.get_barrier_semaphore(), count)

    gather(
        me,
        left_own,
        right_own,
        half,
        half_wide,
        mine_send,
        mine,
        every,
        wide,
        (g_send, g_first, g_next, g_twin, g_left),
    )
    outer_sums(mine, half_wide, wide, stack)
    left_gates(
        out_w,
        pair_wide,
        turned_all.at[1],
        turned_all.at[0],
        stack,
        mid_all,
        normed_all,
        acc.at[0],
        left_side,
    )
    spread(
        me,
        left_side,
        right_side,
        lambda: right_gates(
            turned_all.at[3], turned_all.at[2], normed_all, acc.at[1], right_side
        ),
        lambda: output_gates(turned_all.at[4], normed_all, gate_all),
        a_out,
        rows_all,
        b_all,
        b_out,
        (ly_mid, lz_mid, ry_mid, rz_mid),
        (l_send, l_first, l_z, l_s),
        (r_send, r_first, r_z, r_s),
        (x_send, x_near, x_far, x_side),
    )
    multiply_and_return(
        me, rows_all, b_out, cols_all, product, py_mid, pz_mid, final, (p_send, p_first, p_final)
    )
    finish(final, acc.at[0], mid_all, gate_all, turned_all.at[5], rows_out, result, out_sem)
    legs_left(ly_mid, lz_mid, l_send)
    legs_left(ry_mid, rz_mid, r_send)
    await_bytes(a_out.at[:, pl.ds(0, 2)], x_send.at[0])
    await_bytes(a_out.at[:, 0], x_send.at[1])
    await_bytes(b_out.at[:, pl.ds(0, NX - 1)], x_send.at[2])
    legs_left(py_mid, pz_mid, p_send)


def on_device(pair, alignment, opm_left, opm_right, opm_out, *weights):
    rows, cols, width = pair.shape
    model = alignment.shape[2]
    factor = opm_left.shape[1]
    hidden = weights[0].shape[1]
    seqs = NZ * NS

    def vb(*shape):
        return pltpu.VMEM(shape, BF16)

    def vf(*shape):
        return pltpu.VMEM(shape, F32)

    scratch = [
        vb(rows, cols, width),
        vb(factor * factor, width),
        vf(factor * factor, width),
        vb(width, factor * factor),
        vf(model // 128, cols, 128),
        vb(2, NS, rows * factor),
        vb(factor, cols),
        vb(NZ, NS, rows * factor),
        vf(2, seqs, 128),
        vb(NS, NZ, rows * factor),
        vb(NS, NZ, rows * factor),
        vb(NZ, NY, 2, factor, cols),
        vf(2, seqs * factor, 128),
        vb(rows, factor * factor, cols),
        vb(rows, width, cols),
        vb(rows, width, cols),
        vf(2, 2, hidden * rows, 128),
        vb(2, NZ, NS, rows, 128),
        vb(2, NZ, NS, rows, 128),
        vb(NS, NZ, rows, 128),
        vb(NZ, NS, rows, 128),
        vb(NS, NZ, rows, 128),
        vb(NZ, NS, rows, 128),
        vb(NS, NZ, rows, 128),
        vb(NZ, NS, rows, 128),
        vb(2, NZ, NS, rows, 128),
        vb(2, NX, NZ, NS, rows, 128),
        vb(NZ, NS * rows, NX * cols),
        vb(2, NX, NZ // NX, NS, rows, 128),
        vb(cols, NX * cols),
        vb(2, NZ, NS, rows, 128),
        vb(2, NZ, NS, rows, 128),
        vf(rows, width, cols),
        vb(rows, cols, width),
        vf(rows, width, cols),
        vb(6, hidden, width),
        DMA((2,)),
        DMA((5,)),
        DMA,
        DMA((8, 2)),
        DMA((8, 2)),
        DMA((2,)),
        DMA((4,)),
        DMA((2,)),
        DMA((NZ,)),
        DMA((NS,)),
        DMA((4,)),
        DMA((2,)),
        DMA((NZ,)),
        DMA((NS,)),
        DMA((3,)),
        DMA((2, UNITS)),
        DMA((UNITS,)),
        DMA,
        DMA((4,)),
        DMA((2, 2)),
        DMA,
        DMA,
    ]
    return pl.pallas_call(
        kernel,
        out_shape=jax.ShapeDtypeStruct((rows, cols, width), BF16),
        in_specs=[ANY, ANY] + [VMEM] * 9,
        out_specs=ANY,
        scratch_shapes=scratch,
        compiler_params=pltpu.CompilerParams(
            collective_id=0, has_side_effects=True, vmem_limit_bytes=56 << 20
        ),
        name="evoformer_pair",
    )(pair, opm_out, alignment, opm_left.T, opm_right.T, *weights)


def solution(mesh):
    split = P(("row", "seq"), "col", None)
    return jax.shard_map(
        on_device,
        mesh=mesh,
        in_specs=(split, split) + (P(),) * 9,
        out_specs=split,
        check_vma=False,
    )
```

```python
import jax
import jax.numpy as jnp
from jax import lax
from jax.experimental import pallas as pl
from jax.experimental.pallas import tpu as pltpu
from jax.sharding import PartitionSpec as P

EPS = 1e-05
MESH = pl.DeviceIdType.MESH
F32 = jnp.float32
BF16 = jnp.bfloat16
VMEM = pl.BlockSpec(memory_space=pltpu.VMEM)
ANY = pl.BlockSpec(memory_space=pl.ANY)
DMA = pltpu.SemaphoreType.DMA

NX = 4
NZ = 8
NQ = 8
NS = 2 * NQ
NY = NS // 2
HOPS = (1, 7, 2, 6, 3, 5, 4)


class Place:
    def __init__(self):
        row = lax.axis_index("row")
        self.x = lax.axis_index("col")
        seq = lax.axis_index("seq")
        self.z = row // 2
        self.s = (row % 2) * NQ + seq
        self.yy = self.s // 2
        self.core = self.s % 2

    def at(self, z=None, s=None, x=None):
        z = self.z if z is None else z
        s = self.s if s is None else s
        x = self.x if x is None else x
        return (z * 2 + s // NQ, x, s % NQ)


def send(src, dst, send_sem, recv_sem, device):
    pltpu.make_async_remote_copy(
        src_ref=src,
        dst_ref=dst,
        send_sem=send_sem,
        recv_sem=recv_sem,
        device_id=device,
        device_id_type=MESH,
    ).start()


def keep(src, dst, sem):
    pltpu.make_async_copy(src, dst, sem).start()


def await_bytes(ref, sem):
    pltpu.make_async_copy(ref, ref, sem).wait()


def greet(device):
    pl.semaphore_signal(
        pltpu.get_barrier_semaphore(), inc=1, device_id=device, device_id_type=MESH
    )


def layer_norm(values, axis):
    values = values.astype(F32)
    center = values - jnp.mean(values, axis=axis, keepdims=True)
    spread = jnp.mean(center * center, axis=axis, keepdims=True)
    return center * lax.rsqrt(spread + EPS)


def turned(ref):
    return ref[...].astype(F32).T.astype(BF16)


def dot(a, b):
    return jnp.dot(a, b, preferred_element_type=F32)


def lanes(h):
    return slice(h * 128, (h + 1) * 128)


def flat_rows(ref):
    values = ref[...].astype(F32)
    return values.reshape(-1, values.shape[-1]).astype(BF16)


def split_rows(values):
    return values.reshape(-1, 8, values.shape[-1]).astype(BF16)


def factors(align_ref, wl_ref, wr_ref, normed, left_own, right_own):
    cols, width = align_ref.shape[1:]
    p = wl_ref.shape[0]
    seq = layer_norm(align_ref[0], 1).astype(BF16)
    right_own[...] = lax.dot_general(
        wr_ref[...], seq, (((1,), (1,)), ((), ())), preferred_element_type=F32
    ).astype(BF16)
    wide = seq.astype(F32)
    for h in range(width // 128):
        normed[h] = wide[:, lanes(h)]
    lane = lax.broadcasted_iota(jnp.int32, (p, 8 * p), 1)
    unit = lax.broadcasted_iota(jnp.int32, (p, 8 * p), 0)
    tile = jnp.where(lane % p == unit, 1.0, 0.0).astype(BF16)
    repeated = dot(turned(wl_ref), tile)
    group = lax.broadcasted_iota(jnp.int32, repeated.shape, 1) // p
    total = None
    for i in range(8):
        rows = jnp.concatenate(
            [normed[h, pl.ds(i, cols // 8, stride=8), :] for h in range(width // 128)], axis=1
        ).astype(BF16)
        term = dot(rows, jnp.where(group == i, repeated, 0.0).astype(BF16))
        total = term if total is None else total + term
    left_own[...] = total.astype(BF16).reshape(left_own.shape)


def greet_all(me):
    for t in range(1, NS):
        greet(me.at(s=(me.s + t) % NS))
    for t in range(1, NZ):
        greet(me.at(z=(me.z + t) % NZ))
    for t in range(1, NX):
        greet(me.at(x=(me.x + t) % NX))
    owner = me.z // 2
    for t in range(NZ):

        @pl.when(jnp.logical_not(jnp.logical_and(owner == me.x, me.z == t)))
        def _():
            greet(me.at(z=t, x=owner))

    return NS - 1 + NZ - 1 + NX - 1 + 8 - jnp.where(owner == me.x, 1, 0)


def gather(me, left_own, right_own, half, half_wide, mine_send, mine, every, wide, sems):
    send_sem, first_sem, next_sem, twin_sem, left_sem = sems
    z, s, x, yy, core = me.z, me.s, me.x, me.yy, me.core
    q = right_own.shape[0]
    here = jnp.where(z // 2 == x, 1, 0)

    own = every.at[z, yy, core]
    keep(right_own, own, first_sem)

    @pl.when(core == 0)
    def _():
        for t in HOPS:
            send(right_own, own, send_sem.at[1], first_sem, me.at(z=(z + t) % NZ))

    @pl.when(core == 1)
    def _():
        for t in HOPS:
            send(right_own, own, send_sem.at[1], first_sem, me.at(s=(s + 2 * t) % NS))

    for h in range(2):
        for xt in range(NX):
            zt = 2 * x + h
            same = jnp.logical_and(x == xt, z == zt)

            @pl.when(same)
            def _():
                keep(left_own.at[h], half.at[z], left_sem.at[0])

            @pl.when(jnp.logical_not(same))
            def _():
                send(left_own.at[h], half.at[z], send_sem.at[0], left_sem.at[0], me.at(z=zt, x=xt))

    await_bytes(every.at[:, 0, 0], first_sem)
    twin = me.at(s=s + 1 - 2 * core)

    def line(c, p, half_line):
        at = pl.ds(4 * half_line, 4)
        return every.at[at, index_of(c, p), 0] if c == 0 else every.at[index_of(c, p), at, 1]

    def index_of(c, p):
        return p % 2 * 4 + p // 2 if c == 0 else p

    def place_of(c):
        return yy % 4 * 2 + yy // 4 if c == 0 else z

    def peer(c, p):
        return me.at(s=2 * index_of(c, p)) if c == 0 else me.at(z=p)

    def widen(c, p, half_line):
        @pl.loop(0, 4)
        def _(j):
            n = (4 * half_line + j) * NS + 2 * index_of(c, p)
            if c == 1:
                n = index_of(c, p) * NS + 2 * (4 * half_line + j) + 1
            at = pl.ds(pl.multiple_of(n * q, q), q)
            block = line(c, p, half_line)[j].astype(F32)
            for h in range(2):
                wide[h, at, :] = block[:, lanes(h)]

    events = [
        (d, way, half_line)
        for d in (2, 1, 3, 4)
        for half_line in range(2)
        for way in range(2)
        if d <= 3 + (way == half_line)
    ]

    def moved(c, d, way):
        return (place_of(c) + (NZ - d if way == 0 else d)) % NZ

    for c in range(2):

        @pl.when(core == c)
        def _(c=c):
            here_p = place_of(c)
            for step, half_line in ((2, 0), (2, 1), (1, 0), (1, 1)):
                part = line(c, here_p, half_line)
                for end in (step, NZ - step):
                    send(
                        part,
                        part,
                        send_sem.at[3],
                        next_sem.at[index_of(c, here_p), half_line],
                        peer(c, (here_p + end) % NZ),
                    )
            for half_line in range(2):
                part = line(c, here_p, half_line)
                send(
                    part,
                    part,
                    send_sem.at[4],
                    twin_sem.at[index_of(c, here_p), half_line],
                    twin,
                )

    await_bytes(half, left_sem.at[0])
    for h in range(2):
        half_wide[h] = half[:, :, lanes(h)].astype(F32).reshape(NZ * NS, 128)
    for b in range(NS):
        mine_send[b] = jnp.concatenate(
            [half_wide[h, pl.ds(b, NZ, stride=NS), :] for h in range(2)], axis=1
        ).astype(BF16)
    keep(mine_send.at[s], mine.at[s], left_sem.at[1])
    for t in range(1, NS):
        st = (s + t) % NS
        send(mine_send.at[st], mine.at[s], send_sem.at[2], left_sem.at[1], me.at(s=st))

    for c in range(2):

        @pl.when(core == c)
        def _(c=c):
            here_p = place_of(c)
            steps = [(here_p, 0, 0, 0), (here_p, 0, 0, 1)] + [
                (moved(c, d, way), d, way, half_line) for d, way, half_line in events
            ]
            far_p = place_of(1 - c)
            far_steps = [(far_p, 0), (far_p, 1)] + [
                (moved(1 - c, d, way), half_line) for d, way, half_line in events
            ]

            def from_twin(k):
                p, half_line = far_steps[k]
                part = line(1 - c, p, half_line)
                await_bytes(part, twin_sem.at[index_of(1 - c, p), half_line])
                widen(1 - c, p, half_line)

            for k, (p, d, way, half_line) in enumerate(steps):
                part = line(c, p, half_line)
                if d:
                    sem = next_sem.at[index_of(c, p), half_line]
                    await_bytes(part, sem)
                    if d == 2:
                        for more in range(1, 2 + (way == half_line)):
                            end = (here_p + (NZ - more if way else more)) % NZ
                            send(part, part, send_sem.at[3], sem, peer(c, end))
                    send(
                        part,
                        part,
                        send_sem.at[4],
                        twin_sem.at[index_of(c, p), half_line],
                        twin,
                    )
                widen(c, p, half_line)
                if k >= 4:
                    from_twin(k - 4)
            for k in range(len(steps) - 4, len(steps)):
                from_twin(k)

    await_bytes(mine, left_sem.at[1])

    @pl.when(here == 1)
    def _():
        await_bytes(half.at[pl.ds(0, 7)], send_sem.at[0])

    @pl.when(here == 0)
    def _():
        await_bytes(half, send_sem.at[0])

    await_bytes(every.at[pl.ds(0, 7), 0, 0], send_sem.at[1])
    await_bytes(mine.at[pl.ds(0, NS - 1)], send_sem.at[2])
    await_bytes(every.at[pl.ds(0, 7), :, 0], send_sem.at[3])
    await_bytes(every.at[:, :, 0], send_sem.at[4])


def outer_sums(mine, mine_wide, wide, stack):
    rows, factor, cols = stack.shape[0], mine.shape[2] // stack.shape[0], stack.shape[2]
    seqs = NZ * NS
    for h in range(2):
        mine_wide[h] = mine[:, :, lanes(h)].astype(F32).reshape(seqs, 128)
    left = jnp.concatenate(
        [
            jnp.concatenate(
                [mine_wide[h, pl.ds(z, NS, stride=NZ), :] for z in range(NZ)], axis=0
            ).T
            for h in range(2)
        ],
        axis=0,
    )
    left = (left * (1.0 / seqs)).astype(BF16)

    @pl.loop(0, factor, unroll=4)
    def _(q):
        part = jnp.concatenate(
            [wide[h, pl.ds(q, seqs, stride=factor), :] for h in range(2)], axis=1
        ).astype(BF16)
        outer = dot(left, part)
        at = pl.ds(pl.multiple_of(q * factor, factor), factor)
        stack[:, at, :] = outer.astype(BF16).reshape(rows, factor, cols)


def gated(gate, value, normed, acc, i):
    rows = acc.shape[1] // value.shape[0]
    side = jax.nn.sigmoid(dot(gate, normed)) * dot(value, normed)
    for h in range(2):
        acc[h, pl.ds(i, value.shape[0], stride=rows), :] = side[:, lanes(h)]


def put_side(acc, side):
    for h in range(2):
        side[h] = split_rows(acc[h]).reshape(side.shape[1:])


def left_gates(out_w, pair, gate, value, stack, mid_all, normed_all, acc, side):
    gate, value = gate[...], value[...]

    @pl.loop(0, pair.shape[0], unroll=2)
    def _(i):
        mid = (dot(out_w[...], stack[i]) + pair[i]).astype(BF16)
        mid_all[i] = mid
        normed = layer_norm(mid, 0).astype(BF16)
        normed_all[i] = normed
        gated(gate, value, normed, acc, i)

    put_side(acc, side)


def right_gates(gate, value, normed_all, acc, side):
    gate, value = gate[...], value[...]

    @pl.loop(0, normed_all.shape[0], unroll=2)
    def _(i):
        gated(gate, value, normed_all[i], acc, i)

    put_side(acc, side)


def along_y(me, src, dst, send_sem, sem, offsets=range(NS)):
    for t in offsets:
        if t == 0:
            keep(src(me.s), dst, sem)
        else:
            st = (me.s + t) % NS
            send(src(st), dst, send_sem, sem, me.at(s=st))


def along_z(me, src, dst, send_sem, sem, offsets=(0,) + HOPS):
    for t in offsets:
        if t == 0:
            keep(src(me.z), dst, sem)
        else:
            zt = (me.z + t) % NZ
            send(src(zt), dst, send_sem, sem, me.at(z=zt))


ORDER = (0,) + HOPS
UNITS = NZ + NS
LAG = 8


def left_legs(me, side, y_mid, z_mid, out, sems):
    send_sem, first_sem, z_sem, s_sem = sems
    await_bytes(y_mid, first_sem.at[0])
    along_z(me, lambda zt: y_mid.at[:, zt], out.at[0, me.z], send_sem.at[2], z_sem.at[me.z])
    await_bytes(z_mid, first_sem.at[1])
    along_y(me, lambda st: z_mid.at[:, st], out.at[1, :, me.s], send_sem.at[3], s_sem.at[me.s])


def first_legs(me, side, y_mid, z_mid, send_sem, first_sem, parts=(0, 1)):
    for part in parts:
        along_y(
            me,
            lambda st: side.at[0, :, st],
            y_mid.at[me.s],
            send_sem.at[0],
            first_sem.at[0],
            range(part, NS, 2),
        )
        along_z(
            me,
            lambda zt: side.at[1, zt],
            z_mid.at[me.z],
            send_sem.at[1],
            first_sem.at[1],
            ORDER[4 * part : 4 * part + 4],
        )


def legs_left(y_mid, z_mid, send_sem):
    await_bytes(y_mid.at[pl.ds(0, NS - 1)], send_sem.at[0])
    await_bytes(z_mid.at[pl.ds(0, NZ - 1)], send_sem.at[1])
    await_bytes(y_mid.at[:, pl.ds(0, NZ - 1)], send_sem.at[2])
    await_bytes(z_mid.at[:, pl.ds(0, NS - 1)], send_sem.at[3])


def spread(
    me, left_side, right_side, right_gates, output_gates, a_out, rows_all, b_all, b_out, mids, l_sems, r_sems, x_sems
):
    z, s, x = me.z, me.s, me.x
    ly_mid, lz_mid, ry_mid, rz_mid = mids
    x_send, near_sem, far_sem, side_sem = x_sems
    first_legs(me, left_side, ly_mid, lz_mid, l_sems[0], l_sems[1])
    right_gates()
    first_legs(me, right_side, ry_mid, rz_mid, r_sems[0], r_sems[1], (0,))
    output_gates()
    left_legs(me, left_side, ly_mid, lz_mid, a_out.at[:, x], l_sems)
    first_legs(me, right_side, ry_mid, rz_mid, r_sems[0], r_sems[1], (1,))

    after, before = (x + 1) % NX, (x + 3) % NX

    def unit(k):
        if k < NZ:
            zt = (z + ORDER[k]) % NZ
            return zt, lambda xt: a_out.at[0, xt, zt], l_sems[2].at[zt]
        st = (s + 2 * NS - k + NZ) % NS
        return NZ + st, lambda xt: a_out.at[1, xt, :, st], l_sems[3].at[st]

    def pass_on(k):
        n, place, _ = unit(k)
        way = k % 2
        part = place(after if way else before)
        await_bytes(part, near_sem.at[way, n])
        send(part, part, x_send.at[1], far_sem.at[n], me.at(x=before if way else after))

    for k in range(UNITS):
        n, place, sem = unit(k)
        part = place(x)
        await_bytes(part, sem)
        send(part, part, x_send.at[0], near_sem.at[0, n], me.at(x=after))
        send(part, part, x_send.at[0], near_sem.at[1, n], me.at(x=before))
        if k >= LAG:
            pass_on(k - LAG)
        if k == UNITS - 8:
            left_legs(me, right_side, ry_mid, rz_mid, b_all, r_sems)
    for k in range(UNITS - LAG, UNITS):
        pass_on(k)

    for k in range(NZ):
        zt = (z + ORDER[k]) % NZ
        xt = zt // 2
        part, there = b_all.at[0, zt], b_out.at[0, x, zt % 2]
        await_bytes(part, r_sems[2].at[zt])

        @pl.when(xt == x)
        def _():
            keep(part, there, side_sem)

        @pl.when(xt != x)
        def _():
            send(part, there, x_send.at[2], side_sem, me.at(x=xt))

        for u in (2 * k, 2 * k + 1):
            su = (s + NS - u) % NS
            await_bytes(b_all.at[1, :, su], r_sems[3].at[su])
            for d in (1, 3, 2):
                xt = (x + d) % NX
                send(
                    b_all.at[1, pl.ds(2 * xt, 2), su],
                    b_out.at[1, x, :, su],
                    x_send.at[2],
                    side_sem,
                    me.at(x=xt),
                )
    keep(b_all.at[1, pl.ds(2 * x, 2)], b_out.at[1, x], side_sem)

    for k in range(UNITS):
        n, place, _ = unit(k)
        part = place(x)
        await_bytes(part, far_sem.at[n])
        await_bytes(part, near_sem.at[1 - k % 2, n])

    @pl.loop(0, NZ)
    def _(zt):
        for k in range(NX):
            for h in range(2):
                rows_all[zt, :, lanes(2 * k + h)] = flat_rows(a_out.at[h, k, zt])

    await_bytes(b_out, side_sem)


def multiply_and_return(me, rows_all, b_out, cols_all, product, y_mid, z_mid, final, sems):
    send_sem, first_sem, final_sem = sems
    z, s = me.z, me.s
    for k in range(NX):
        for h in range(2):
            cols_all[:, lanes(2 * k + h)] = flat_rows(b_out.at[h, k])
    for couple in ((0, 1), (7, 2), (6, 3), (5, 4)):
        rows = jnp.concatenate([rows_all[(z + t) % NZ] for t in couple], axis=0)
        total = lax.dot_general(
            rows, cols_all[...], (((1,), (1,)), ((), ())), preferred_element_type=F32
        )
        count = total.shape[0] // 2
        for n, t in enumerate(couple):
            zt = (z + t) % NZ
            block = total[n * count : (n + 1) * count]
            for h in range(2):
                product[h, zt] = split_rows(block[:, lanes(h)])
    same = s // NQ * NQ
    starts = (same, NQ - same)

    def first(chunk):
        near = pl.ds(pl.multiple_of(starts[chunk], NQ), NQ)
        along_z(
            me,
            lambda zt: product.at[1, zt, near],
            z_mid.at[z, near],
            send_sem.at[1],
            first_sem.at[1, chunk],
        )
        for t in range(chunk, NZ, 2):
            zt = (z + t) % NZ
            along_y(
                me,
                lambda st: product.at[0, zt, st],
                y_mid.at[s, zt],
                send_sem.at[0],
                first_sem.at[0, chunk],
            )

    def second(chunk):
        await_bytes(z_mid.at[:, pl.ds(0, NQ)], first_sem.at[1, chunk])
        base = starts[chunk]
        for t in range(NQ):
            st = base + (s + t) % NQ
            part, there = z_mid.at[:, st], final.at[1, :, s]
            if t == 0 and chunk == 0:
                keep(part, there, final_sem)
            else:
                send(part, there, send_sem.at[3], final_sem, me.at(s=st))
        await_bytes(y_mid.at[:, pl.ds(0, NZ // 2)], first_sem.at[0, chunk])
        along_z(
            me,
            lambda zt: y_mid.at[:, zt],
            final.at[0, z],
            send_sem.at[2],
            final_sem,
            (0, 2, 6, 4) if chunk == 0 else (1, 7, 3, 5),
        )

    first(0)
    first(1)
    second(0)
    second(1)
    await_bytes(final, final_sem)


def output_gates(gate, normed_all, gate_all):
    gate = gate[...]

    @pl.loop(0, normed_all.shape[0], unroll=2)
    def _(i):
        gate_all[i] = jax.nn.sigmoid(dot(gate, normed_all[i]))


def finish(parts, wide, mid_all, gate_all, out_w, result):
    rows, width, cols = mid_all.shape
    for h in range(2):
        wide[h] = parts[h].astype(F32).reshape(-1, 128)
    hidden = wide.shape[1] // rows
    out_w = out_w[...]

    @pl.loop(0, rows, unroll=4)
    def _(i):
        product = jnp.concatenate(
            [wide[h, pl.ds(i, hidden, stride=rows), :] for h in range(2)], axis=1
        )
        normed = layer_norm(product, 0).astype(BF16)
        update = gate_all[i] * dot(out_w, normed)
        result[i] = (mid_all[i].astype(F32) + update).T.astype(BF16)


def kernel(
    pair_hbm,
    opm_out_hbm,
    align_ref,
    opm_left_ref,
    opm_right_ref,
    tri_left_ref,
    tri_left_gate_ref,
    tri_right_ref,
    tri_right_gate_ref,
    tri_gate_ref,
    tri_out_ref,
    result,
    pair,
    opm_out,
    opm_wide,
    out_w,
    normed_seq,
    left_own,
    right_own,
    half,
    half_wide,
    mine_send,
    mine,
    every,
    wide,
    stack,
    mid_all,
    normed_all,
    acc,
    left_side,
    right_side,
    ly_mid,
    lz_mid,
    ry_mid,
    rz_mid,
    py_mid,
    pz_mid,
    b_all,
    a_out,
    rows_all,
    b_out,
    cols_all,
    product,
    final,
    gate_all,
    pair_wide,
    turned_all,
    load_sem,
    g_send,
    g_first,
    g_next,
    g_twin,
    g_left,
    l_send,
    l_first,
    l_z,
    l_s,
    r_send,
    r_first,
    r_z,
    r_s,
    x_send,
    x_near,
    x_far,
    x_side,
    p_send,
    p_first,
    p_final,
):
    me = Place()
    count = greet_all(me)
    keep(pair_hbm, pair, load_sem.at[0])
    keep(opm_out_hbm, opm_out, load_sem.at[1])
    factors(align_ref, opm_left_ref, opm_right_ref, normed_seq, left_own, right_own)
    await_bytes(opm_out, load_sem.at[1])
    await_bytes(pair, load_sem.at[0])
    opm_wide[...] = opm_out[...].astype(F32)
    p = opm_left_ref.shape[0]
    q = opm_right_ref.shape[0]
    for k in range(q):
        rows = opm_wide[pl.ds(k, p, stride=q), :]
        mine_rows = slice(k * p, (k + 1) * p)
        stack[0, mine_rows, 0:128] = rows.astype(BF16)
    out_w[...] = stack[0, :, 0:128].astype(F32).T.astype(BF16)
    for k, ref in enumerate(
        (
            tri_left_ref,
            tri_left_gate_ref,
            tri_right_ref,
            tri_right_gate_ref,
            tri_gate_ref,
            tri_out_ref,
        )
    ):
        turned_all[k] = turned(ref)

    @pl.loop(0, pair.shape[0])
    def _(i):
        pair_wide[i] = pair[i].astype(F32).T

    pl.semaphore_wait(pltpu.get_barrier_semaphore(), count)

    gather(
        me,
        left_own,
        right_own,
        half,
        half_wide,
        mine_send,
        mine,
        every,
        wide,
        (g_send, g_first, g_next, g_twin, g_left),
    )
    outer_sums(mine, half_wide, wide, stack)
    left_gates(
        out_w,
        pair_wide,
        turned_all.at[1],
        turned_all.at[0],
        stack,
        mid_all,
        normed_all,
        acc.at[0],
        left_side,
    )
    spread(
        me,
        left_side,
        right_side,
        lambda: right_gates(
            turned_all.at[3], turned_all.at[2], normed_all, acc.at[1], right_side
        ),
        lambda: output_gates(turned_all.at[4], normed_all, gate_all),
        a_out,
        rows_all,
        b_all,
        b_out,
        (ly_mid, lz_mid, ry_mid, rz_mid),
        (l_send, l_first, l_z, l_s),
        (r_send, r_first, r_z, r_s),
        (x_send, x_near, x_far, x_side),
    )
    multiply_and_return(
        me, rows_all, b_out, cols_all, product, py_mid, pz_mid, final, (p_send, p_first, p_final)
    )
    finish(final, acc.at[0], mid_all, gate_all, turned_all.at[5], result)
    legs_left(ly_mid, lz_mid, l_send)
    legs_left(ry_mid, rz_mid, r_send)
    await_bytes(a_out.at[:, pl.ds(0, 2)], x_send.at[0])
    await_bytes(a_out.at[:, 0], x_send.at[1])
    await_bytes(b_out.at[:, pl.ds(0, NX - 1)], x_send.at[2])
    legs_left(py_mid, pz_mid, p_send)


def on_device(pair, alignment, opm_left, opm_right, opm_out, *weights):
    rows, cols, width = pair.shape
    model = alignment.shape[2]
    factor = opm_left.shape[1]
    hidden = weights[0].shape[1]
    seqs = NZ * NS

    def vb(*shape):
        return pltpu.VMEM(shape, BF16)

    def vf(*shape):
        return pltpu.VMEM(shape, F32)

    scratch = [
        vb(rows, cols, width),
        vb(factor * factor, width),
        vf(factor * factor, width),
        vb(width, factor * factor),
        vf(model // 128, cols, 128),
        vb(2, NS, rows * factor),
        vb(factor, cols),
        vb(NZ, NS, rows * factor),
        vf(2, seqs, 128),
        vb(NS, NZ, rows * factor),
        vb(NS, NZ, rows * factor),
        vb(NZ, NY, 2, factor, cols),
        vf(2, seqs * factor, 128),
        vb(rows, factor * factor, cols),
        vb(rows, width, cols),
        vb(rows, width, cols),
        vf(2, 2, hidden * rows, 128),
        vb(2, NZ, NS, rows, 128),
        vb(2, NZ, NS, rows, 128),
        vb(NS, NZ, rows, 128),
        vb(NZ, NS, rows, 128),
        vb(NS, NZ, rows, 128),
        vb(NZ, NS, rows, 128),
        vb(NS, NZ, rows, 128),
        vb(NZ, NS, rows, 128),
        vb(2, NZ, NS, rows, 128),
        vb(2, NX, NZ, NS, rows, 128),
        vb(NZ, NS * rows, NX * cols),
        vb(2, NX, NZ // NX, NS, rows, 128),
        vb(cols, NX * cols),
        vb(2, NZ, NS, rows, 128),
        vb(2, NZ, NS, rows, 128),
        vf(rows, width, cols),
        vf(rows, width, cols),
        vb(6, hidden, width),
        DMA((2,)),
        DMA((5,)),
        DMA,
        DMA((8, 2)),
        DMA((8, 2)),
        DMA((2,)),
        DMA((4,)),
        DMA((2,)),
        DMA((NZ,)),
        DMA((NS,)),
        DMA((4,)),
        DMA((2,)),
        DMA((NZ,)),
        DMA((NS,)),
        DMA((3,)),
        DMA((2, UNITS)),
        DMA((UNITS,)),
        DMA,
        DMA((4,)),
        DMA((2, 2)),
        DMA,
    ]
    return pl.pallas_call(
        kernel,
        out_shape=pltpu.VMEM((rows, cols, width), BF16),
        in_specs=[ANY, ANY] + [VMEM] * 9,
        out_specs=VMEM,
        scratch_shapes=scratch,
        compiler_params=pltpu.CompilerParams(
            collective_id=0, has_side_effects=True, vmem_limit_bytes=56 << 20
        ),
        name="evoformer_pair",
    )(pair, opm_out, alignment, opm_left.T, opm_right.T, *weights)


def solution(mesh):
    split = P(("row", "seq"), "col", None)
    return jax.shard_map(
        on_device,
        mesh=mesh,
        in_specs=(split, split) + (P(),) * 9,
        out_specs=split,
        check_vma=False,
    )
```
